128 devices in a mesh: rows: 8 (over z, core), cols: 16 (over y, x).
Axes of the slice: x: 4, y: 4, z: 4, core: 2. Of those that a mesh axis runs over, the one named last changes fastest.
Arguments:
- m_start: float32 [3, 64, 64, 4096], P(None, 'cols', 'rows'), may hold values from -1 to 1, as said below
- boundary_matrix: bfloat16 [24576, 24576], P('rows', 'cols'), may hold values from -0.0390625 to 0.0390625
- trace_slot: int32 [24576], replicated, may hold values from 0 to 24575, each once
- return_row: int32 [24576], replicated, may hold values from 0 to 24575, each once
Outputs:
- m_final: float32 [3, 64, 64, 4096], P(None, 'cols', 'rows')
The draws below stay inside these ranges and needn't reach their ends.
Inputs may be any that keep to these rules, and one draw needn't show every extreme that they name: `m_start`: every node of every image holds a unit vector over the first dimension. `trace_slot`: a permutation of the 24576 face slots. `return_row`: a permutation of the 24576 boundary rows.
All inputs are finite; a program needn't handle non-finite values.
Results may differ from the reference program's by a relative error of at most 0.00034.
Values may be sent and summed in bfloat16 or wider, within the bound.
No kernel may reach another device: no remote copies, remote signals or barrier semaphores. Data moves between devices by JAX's collectives and lax.ppermute only.
A program may use at most 128 MiB of HBM per device.

```python
import math
import jax
import jax.numpy as jnp
from jax import lax

GRID = 64
STEPS = 2
IMAGES = 64
NB = 24576


def draw_m_start(key, part):
    keys = jax.random.split(jax.random.fold_in(key, 11), 4)
    base = jax.random.normal(keys[0], (3, 1, GRID, GRID * GRID), jnp.float32)
    base = base / jnp.sqrt(jnp.sum(base * base, axis=0, keepdims=True) + 1e-12)
    amplitude = jnp.exp(jax.random.uniform(keys[1], (1, 1, GRID, GRID * GRID), jnp.float32, math.log(0.05), math.log(0.5)))
    ramp = (1.0 + 2.0 * jnp.arange(GRID, dtype=jnp.float32) / (GRID - 1)).reshape(1, 1, GRID, 1)
    level = jnp.exp(jax.random.uniform(keys[2], (1, IMAGES, 1, 1), jnp.float32, math.log(0.3), math.log(3.0)))
    noise = jax.random.normal(keys[3], (3, IMAGES, GRID, GRID * GRID), jnp.float32)
    vectors = base + amplitude * ramp * 0.4 * level * noise
    return vectors / jnp.sqrt(jnp.sum(vectors * vectors, axis=0, keepdims=True) + 1e-12)


def level_of(stream_key, dims, pieces, low, top_value):
    def one(dim, parts):
        heights = jax.random.uniform(jax.random.fold_in(jax.random.fold_in(stream_key, 6), dim), (parts,), jnp.float32, low / len(pieces), top_value / len(pieces))
        return jnp.repeat(jnp.exp(heights), dims[dim] // parts).reshape((-1,) + (1,) * (len(dims) - dim - 1))

    gain = one(*pieces[0])
    for cut in pieces[1:]:
        gain = gain * one(*cut)
    return gain


def centred(stream_key, shape, spread, bound, cuts=(), kind=jnp.bfloat16):
    loudness = level_of(stream_key, shape, cuts, -0.22, 0.18) if cuts else 1.0
    array = jax.random.normal(stream_key, shape, jnp.float32) * spread * loudness
    return jnp.minimum(jnp.maximum(array, -bound), bound).astype(kind)


def setup_inputs(seed: int = 0) -> dict:
    arg_keys = jax.random.split(jax.random.key(seed), 5)
    m_start = draw_m_start(jax.random.fold_in(arg_keys[4], 71), 0)
    boundary_matrix = centred(arg_keys[1], (NB, NB), NB ** -0.5, 0.0390625, ((0, 8), (1, 16)))
    trace_slot = jax.random.permutation(arg_keys[2], NB).astype(jnp.int32)
    return_row = jax.random.permutation(arg_keys[3], NB).astype(jnp.int32)
    return {"m_start": m_start, "boundary_matrix": boundary_matrix, "trace_slot": trace_slot, "return_row": return_row}


exchange_coef = 0.25
demag_coef = 2.0
time_step = 0.2
spring_coef = 2.0

def shift_flat(values, offset):
    filler = jnp.zeros(values.shape[:-1] + (abs(offset),), values.dtype)
    if offset > 0:
        return jnp.concatenate([values[..., offset:], filler], axis=-1)
    return jnp.concatenate([filler, values[..., :offset]], axis=-1)

def stencils(padded, first_plane):
    centre = padded[:, :, 1:-1]
    planes = centre.shape[2]
    plane_at = first_plane + jnp.arange(planes, dtype=jnp.int32)
    upper_open = (plane_at < GRID - 1).astype(jnp.float32).reshape(1, 1, planes, 1)
    lower_open = (plane_at > 0).astype(jnp.float32).reshape(1, 1, planes, 1)
    flat_index = jnp.arange(GRID * GRID, dtype=jnp.int32)
    column_at = flat_index % GRID
    row_at = flat_index // GRID
    east_open = (column_at < GRID - 1).astype(jnp.float32)
    west_open = (column_at > 0).astype(jnp.float32)
    north_open = (row_at < GRID - 1).astype(jnp.float32)
    south_open = (row_at > 0).astype(jnp.float32)
    east_value = shift_flat(centre, 1) * east_open
    west_value = shift_flat(centre, -1) * west_open
    north_value = shift_flat(centre, GRID) * north_open
    south_value = shift_flat(centre, -GRID) * south_open
    upper_value = padded[:, :, 2:] * upper_open
    lower_value = padded[:, :, :-2] * lower_open
    neighbours = east_open + west_open + north_open + south_open + upper_open + lower_open
    laplace = east_value + west_value + north_value + south_value + upper_value + lower_value - neighbours * centre
    diverge = 0.5 * (east_value[0] - west_value[0] + north_value[1] - south_value[1] + upper_value[2] - lower_value[2])
    return (laplace, diverge)

def cycle_values(diverge):
    faces = jnp.stack([diverge[..., :GRID], diverge[..., GRID * GRID - GRID:], diverge[..., ::GRID], diverge[..., GRID - 1::GRID]], axis=2)
    return faces.reshape(diverge.shape[0], -1)

def surface_field(cycle_phi, bottom_phi, top_phi, first_plane):
    images_here = cycle_phi.shape[0]
    planes = cycle_phi.shape[1] // (4 * GRID)
    faces = cycle_phi.reshape(images_here, planes, 4, GRID)
    middle = jnp.zeros((images_here, planes, GRID * GRID - 2 * GRID), cycle_phi.dtype)
    field_y = jnp.concatenate([faces[:, :, 0], middle, -faces[:, :, 1]], axis=-1)
    column_at = jnp.arange(GRID * GRID, dtype=jnp.int32) % GRID
    field_x = jnp.where(column_at == 0, jnp.repeat(faces[:, :, 2], GRID, axis=-1), 0.0) - jnp.where(column_at == GRID - 1, jnp.repeat(faces[:, :, 3], GRID, axis=-1), 0.0)
    plane_at = (first_plane + jnp.arange(planes, dtype=jnp.int32)).reshape(1, planes, 1)
    field_z = jnp.where(plane_at == 0, bottom_phi[:, None, :], 0.0) - jnp.where(plane_at == GRID - 1, top_phi[:, None, :], 0.0)
    return jnp.stack([field_x, field_y, field_z], axis=0)

def torque_step(magnet, field):
    along = lax.optimization_barrier(jnp.sum(magnet * field, axis=0, keepdims=True))
    length = lax.optimization_barrier(jnp.sum(magnet * magnet, axis=0, keepdims=True))
    moved = magnet - time_step * (magnet * along - field * length)
    return moved / jnp.sqrt(lax.optimization_barrier(jnp.sum(moved * moved, axis=0, keepdims=True)))

def tension_step(torqued, tangent, tangent_sq, coefficient, inner):
    entries = 3.0 * GRID * GRID * GRID
    scale = coefficient / jnp.sqrt(tangent_sq / entries + 1e-06)
    force = tangent * scale.reshape(1, -1, 1, 1)
    along = lax.optimization_barrier(jnp.sum(force * torqued, axis=0, keepdims=True))
    pushed = torqued + force - along * torqued
    moved = pushed / jnp.sqrt(lax.optimization_barrier(jnp.sum(pushed * pushed, axis=0, keepdims=True)))
    return jnp.where(inner.reshape(1, -1, 1, 1), moved, torqued)

def reference(m_start, boundary_matrix, trace_slot, return_row):
    magnet = m_start
    images = magnet.shape[1]
    cycle_size = 4 * GRID * GRID
    plane_size = GRID * GRID
    entries = 3.0 * GRID * GRID * GRID
    row_blocks = boundary_matrix.reshape(8, NB // 8, NB)
    for repeat_at in range(STEPS):
        padded = jnp.pad(magnet, ((0, 0), (0, 0), (1, 1), (0, 0)))
        laplace, diverge = stencils(padded, 0)
        surface = jnp.concatenate([cycle_values(diverge), diverge[:, 0], diverge[:, -1]], axis=1).astype(jnp.bfloat16)
        traced = jnp.take(surface, trace_slot, axis=1)

        def product(block_rows):
            return lax.dot_general(traced, block_rows, (((1,), (1,)), ((), ())), preferred_element_type=jnp.float32)
        potential = jnp.transpose(lax.map(product, row_blocks), (1, 0, 2)).reshape(images, NB)
        returned = jnp.take(potential, return_row, axis=1)
        field = exchange_coef * laplace + demag_coef * surface_field(returned[:, :cycle_size], returned[:, cycle_size:cycle_size + plane_size], returned[:, cycle_size + plane_size:], 0)
        torqued = torque_step(magnet, field)
        between = torqued[:, 1:] - torqued[:, :-1]
        spacing = jnp.sqrt(lax.optimization_barrier(jnp.sum(between * between, axis=(0, 2, 3))) / entries + 1e-06)
        tangent = torqued[:, 2:] - torqued[:, :-2]
        tangent_sq = lax.optimization_barrier(jnp.sum(tangent * tangent, axis=(0, 2, 3)))
        coefficient = spring_coef * (spacing[1:] - spacing[:-1])
        inner = jnp.ones((images - 2,), dtype=jnp.bool_)
        middle = tension_step(torqued[:, 1:-1], tangent, tangent_sq, coefficient, inner)
        magnet = jnp.concatenate([torqued[:, :1], middle, torqued[:, -1:]], axis=1)
    return magnet
```

```python
import jax
import jax.numpy as jnp
from jax import lax
from jax.sharding import PartitionSpec as P
from jax.experimental import pallas as pl
from jax.experimental.pallas import tpu as pltpu

GRID = 64
STEPS = 2


exchange_coef = 0.25
demag_coef = 2.0
time_step = 0.2
spring_coef = 2.0
PART = jnp.float32
POT = jnp.float32


def extended_2(cells, sides, width):
    for axis, dim in sides:
        count = lax.axis_size(axis)
        ends = count - 1
        head = lax.slice_in_dim(cells, 0, width, axis=dim)
        tail = lax.slice_in_dim(cells, cells.shape[dim] - width, cells.shape[dim], axis=dim)
        cells = jnp.concatenate(
            [
                lax.ppermute(tail, axis, [(i, (i + 1) % count) for i in range(ends)]),
                cells,
                lax.ppermute(head, axis, [((i + 1) % count, i) for i in range(ends)]),
            ],
            axis=dim,
        )
    return cells


def shift_flat(values, offset):
    filler = jnp.zeros(values.shape[:-1] + (abs(offset),), values.dtype)
    if offset > 0:
        return jnp.concatenate([values[..., offset:], filler], axis=-1)
    return jnp.concatenate([filler, values[..., :offset]], axis=-1)


def stencils(padded, first_plane):
    centre = padded[:, :, 1:-1]
    planes = centre.shape[2]
    plane_at = first_plane + jnp.arange(planes, dtype=jnp.int32)
    upper_open = (plane_at < GRID - 1).astype(jnp.float32).reshape(1, 1, planes, 1)
    lower_open = (plane_at > 0).astype(jnp.float32).reshape(1, 1, planes, 1)
    flat_index = jnp.arange(GRID * GRID, dtype=jnp.int32)
    column_at = flat_index % GRID
    row_at = flat_index // GRID
    east_open = (column_at < GRID - 1).astype(jnp.float32)
    west_open = (column_at > 0).astype(jnp.float32)
    north_open = (row_at < GRID - 1).astype(jnp.float32)
    south_open = (row_at > 0).astype(jnp.float32)
    east_value = shift_flat(centre, 1) * east_open
    west_value = shift_flat(centre, -1) * west_open
    north_value = shift_flat(centre, GRID) * north_open
    south_value = shift_flat(centre, -GRID) * south_open
    upper_value = padded[:, :, 2:] * upper_open
    lower_value = padded[:, :, :-2] * lower_open
    neighbours = east_open + west_open + north_open + south_open + upper_open + lower_open
    laplace = (
        east_value
        + west_value
        + north_value
        + south_value
        + upper_value
        + lower_value
        - neighbours * centre
    )
    diverge = 0.5 * (
        east_value[0]
        - west_value[0]
        + north_value[1]
        - south_value[1]
        + upper_value[2]
        - lower_value[2]
    )
    return (laplace, diverge)


def cycle_values(diverge):
    faces = jnp.stack(
        [
            diverge[..., :GRID],
            diverge[..., GRID * GRID - GRID :],
            diverge[..., ::GRID],
            diverge[..., GRID - 1 :: GRID],
        ],
        axis=2,
    )
    return faces.reshape(diverge.shape[0], -1)


def surface_field(cycle_phi, bottom_phi, top_phi, first_plane):
    images_here = cycle_phi.shape[0]
    planes = cycle_phi.shape[1] // (4 * GRID)
    faces = cycle_phi.reshape(images_here, planes, 4, GRID)
    middle = jnp.zeros((images_here, planes, GRID * GRID - 2 * GRID), cycle_phi.dtype)
    field_y = jnp.concatenate([faces[:, :, 0], middle, -faces[:, :, 1]], axis=-1)
    column_at = jnp.arange(GRID * GRID, dtype=jnp.int32) % GRID
    field_x = jnp.where(column_at == 0, jnp.repeat(faces[:, :, 2], GRID, axis=-1), 0.0) - jnp.where(
        column_at == GRID - 1, jnp.repeat(faces[:, :, 3], GRID, axis=-1), 0.0
    )
    plane_at = (first_plane + jnp.arange(planes, dtype=jnp.int32)).reshape(1, planes, 1)
    field_z = jnp.where(plane_at == 0, bottom_phi[:, None, :], 0.0) - jnp.where(
        plane_at == GRID - 1, top_phi[:, None, :], 0.0
    )
    return jnp.stack([field_x, field_y, field_z], axis=0)


def torque_step(magnet, field):
    along = jnp.sum(magnet * field, axis=0, keepdims=True)
    length = jnp.sum(magnet * magnet, axis=0, keepdims=True)
    moved = magnet - time_step * (magnet * along - field * length)
    return moved / jnp.sqrt(jnp.sum(moved * moved, axis=0, keepdims=True))


def tension_step(torqued, tangent, tangent_sq, coefficient, inner):
    entries = 3.0 * GRID * GRID * GRID
    scale = coefficient / jnp.sqrt(tangent_sq / entries + 1e-06)
    force = tangent * scale.reshape(1, -1, 1, 1)
    along = jnp.sum(force * torqued, axis=0, keepdims=True)
    pushed = torqued + force - along * torqued
    moved = pushed / jnp.sqrt(jnp.sum(pushed * pushed, axis=0, keepdims=True))
    return jnp.where(inner.reshape(1, -1, 1, 1), moved, torqued)


ROWS = 8
COLS = 16
NB = 24576
COL_BLOCK = NB // COLS
ROW_BLOCK = NB // ROWS
CHUNKS = ROW_BLOCK // 256
F32 = jnp.float32
BF16 = jnp.bfloat16


def lane_choice(low):
    lane = lax.broadcasted_iota(jnp.int32, (256, low.shape[1]), 0)
    return jnp.where(lane == low, 1.0, 0.0).astype(BF16)


def trace_kernel(table_ref, low_ref, high_ref, out_ref):
    high = high_ref[0]
    choice = lane_choice(low_ref[0])
    width = high.shape[1]
    plane_in_slab = lax.broadcasted_iota(jnp.int32, (8, width), 0)
    total = [jnp.zeros((8, width), F32) for _ in range(4)]
    for slab in range(ROWS):
        picked = jnp.dot(table_ref[slab, 0:32, :], choice, preferred_element_type=F32)
        mask = (plane_in_slab + 8 * slab) == high
        for p in range(4):
            total[p] = total[p] + jnp.where(mask, picked[8 * p : 8 * p + 8], 0.0)
    for slab, base in ((0, 64), (ROWS - 1, 80)):
        picked = jnp.dot(table_ref[slab, 32:96, :], choice, preferred_element_type=F32)
        for half in range(2):
            mask = (plane_in_slab + (base + 8 * half)) == high
            for p in range(4):
                at = 16 * p + 8 * half
                total[p] = total[p] + jnp.where(mask, picked[at : at + 8], 0.0)
    rows = [jnp.sum(total[p], axis=0, keepdims=True) for p in range(4)]
    out_ref[0] = jnp.concatenate(rows, axis=0).astype(BF16)


def take_trace(table, low, high):
    return pl.pallas_call(
        trace_kernel,
        grid=(COLS,),
        in_specs=[
            pl.BlockSpec((ROWS, 96, 256), lambda i: (0, 0, 0)),
            pl.BlockSpec((1, 1, COL_BLOCK), lambda i: (i, 0, 0)),
            pl.BlockSpec((1, 1, COL_BLOCK), lambda i: (i, 0, 0)),
        ],
        out_specs=pl.BlockSpec((1, 4, COL_BLOCK), lambda i: (i, 0, 0)),
        out_shape=jax.ShapeDtypeStruct((COLS, 4, COL_BLOCK), BF16),
        name="take_trace",
    )(table, low, high)


def partial_kernel(count, ghost, owned_ref, matrix_ref, out_ref, traced_ref, rows_ref, stage_ref):
    @pl.when(pl.program_id(0) == 0)
    def _():
        for c in range(COLS):
            traced_ref[4 * c : 4 * c + 4, :] = owned_ref[c].astype(F32)
        rows_ref[0:8, :] = jnp.zeros((8, 256), F32)
        rows_ref[72:80, :] = jnp.zeros((8, 256), F32)

    traced = traced_ref[...].astype(BF16)
    for part in range(4):
        rows_ref[8:72, :] = lax.dot_general(
            traced,
            matrix_ref[256 * part : 256 * part + 256, :],
            (((1,), (1,)), ((), ())),
            preferred_element_type=F32,
        )
        for c in range(COLS):
            first = 8 + 4 * c - ghost
            stage_ref[c, part * count : part * count + count, :] = rows_ref[first : first + count, :]
    out_ref[...] = stage_ref[...].astype(out_ref.dtype)


def partial_potential(owned, matrix, count, ghost, dtype):
    rows = 4 * count
    return pl.pallas_call(
        lambda *refs: partial_kernel(count, ghost, *refs),
        grid=(3,),
        in_specs=[
            pl.BlockSpec((COLS, 4, COL_BLOCK), lambda i: (0, 0, 0)),
            pl.BlockSpec((1024, COL_BLOCK), lambda i: (i, 0)),
        ],
        out_specs=pl.BlockSpec((COLS, rows, 256), lambda i: (0, i, 0)),
        out_shape=jax.ShapeDtypeStruct((COLS, 3 * rows, 256), dtype),
        scratch_shapes=[
            pltpu.VMEM((64, COL_BLOCK), F32),
            pltpu.VMEM((80, 256), F32),
            pltpu.VMEM((COLS, rows, 256), F32),
        ],
        name="partial_potential",
    )(owned, matrix)


def combine_kernel(count, parts_ref, out_ref, sum_ref):
    total = parts_ref[0].astype(F32)
    for c in range(1, COLS):
        total = total + parts_ref[c].astype(F32)
    sum_ref[0 : CHUNKS * count, :] = total
    rows = jnp.concatenate([sum_ref[count * h : count * h + 8, :] for h in range(CHUNKS)], axis=0)
    for r in range(ROWS):
        out_ref[r] = rows.astype(out_ref.dtype)


def combine(parts, count, dtype):
    return pl.pallas_call(
        lambda *refs: combine_kernel(count, *refs),
        out_shape=jax.ShapeDtypeStruct((ROWS, 8 * CHUNKS, 256), dtype),
        scratch_shapes=[pltpu.VMEM((CHUNKS * count + 8, 256), F32)],
        name="combine",
    )(parts)


def return_kernel(table_ref, low_ref, high_ref, out_ref):
    high = high_ref[0]
    choice = lane_choice(low_ref[0])
    total = jnp.zeros((8, high.shape[1]), F32)
    for slab in range(ROWS):
        table = table_ref[slab]
        if table.dtype == F32:
            top = table.astype(BF16)
            rest = (table - top.astype(F32)).astype(BF16)
            picked = jnp.dot(top, choice, preferred_element_type=F32) + jnp.dot(
                rest, choice, preferred_element_type=F32
            )
        else:
            picked = jnp.dot(table, choice, preferred_element_type=F32)
        for h in range(CHUNKS):
            total = total + jnp.where(
                high == slab * CHUNKS + h, picked[8 * h : 8 * h + 8], 0.0
            )
    out_ref[...] = total


def take_return(table, low, high, tile):
    tiles = low.shape[0]
    return pl.pallas_call(
        return_kernel,
        grid=(tiles,),
        in_specs=[
            pl.BlockSpec((ROWS, 8 * CHUNKS, 256), lambda i: (0, 0, 0)),
            pl.BlockSpec((1, 1, tile), lambda i: (i, 0, 0)),
            pl.BlockSpec((1, 1, tile), lambda i: (i, 0, 0)),
        ],
        out_specs=pl.BlockSpec((8, tile), lambda i: (0, i)),
        out_shape=jax.ShapeDtypeStruct((8, tiles * tile), F32),
        name="take_return",
    )(table, low, high)


def path_step(magnet, boundary_matrix, trace_index, return_index):
    images_here = magnet.shape[1]
    planes = magnet.shape[2]
    cols_count = lax.axis_size("cols")
    rows_at = lax.axis_index("rows")
    cols_at = lax.axis_index("cols")
    first_plane = rows_at * planes
    cycle_size = 4 * planes * GRID
    plane_size = GRID * GRID
    padded = extended_2(magnet, (("rows", 2),), 1)
    laplace, diverge = stencils(padded, first_plane)
    cycle_local = cycle_values(diverge).astype(BF16).reshape(4 * planes, 256)
    own_plane = jnp.where(rows_at == 0, diverge[:, 0], diverge[:, -1]).astype(BF16).reshape(64, 256)
    block = jnp.concatenate([cycle_local, own_plane], axis=0)
    copies = jnp.broadcast_to(block[None], (ROWS, 96, 256))
    table = lax.all_to_all(copies, "rows", split_axis=0, concat_axis=0, tiled=True)
    traced = take_trace(table, *trace_index)
    owned = lax.all_to_all(traced, "cols", split_axis=0, concat_axis=0, tiled=True)
    parts = partial_potential(owned, boundary_matrix, 4, 0, PART)
    parts = lax.all_to_all(parts, "cols", split_axis=0, concat_axis=0, tiled=True)
    mine = combine(parts, 4, POT)
    potential = lax.all_to_all(mine, "rows", split_axis=0, concat_axis=0, tiled=True)
    returned = take_return(potential, *return_index, 512)[:4]
    plane_phi = returned[:, cycle_size:]
    field = exchange_coef * laplace + demag_coef * surface_field(
        returned[:, :cycle_size], plane_phi, plane_phi, first_plane
    )
    torqued = torque_step(magnet, field)
    extended = extended_2(torqued, (("cols", 1),), 1)
    between = extended[:, 1:] - extended[:, :-1]
    tangent = extended[:, 2:] - extended[:, :-2]
    between_sq, tangent_sq = lax.psum(
        (jnp.sum(between * between, axis=(0, 2, 3)), jnp.sum(tangent * tangent, axis=(0, 2, 3))),
        "rows",
    )
    entries = 3.0 * GRID * GRID * GRID
    spacing = jnp.sqrt(between_sq / entries + 1e-06)
    coefficient = spring_coef * (spacing[1:] - spacing[:-1])
    global_image = cols_at * images_here + jnp.arange(images_here, dtype=jnp.int32)
    inner = (global_image >= 1) & (global_image <= images_here * cols_count - 2)
    return tension_step(torqued, tangent, tangent_sq, coefficient, inner)


def body(m_start, boundary_matrix, trace_slot, return_row):
    magnet = m_start
    rows_at = lax.axis_index("rows")
    trace_index = (
        (trace_slot & 255).reshape(COLS, 1, COL_BLOCK),
        (trace_slot >> 8).reshape(COLS, 1, COL_BLOCK),
    )
    own_rows = jnp.concatenate(
        [
            lax.dynamic_slice_in_dim(return_row, rows_at * 2048, 2048),
            jnp.where(rows_at == 0, return_row[16384:20480], return_row[20480:]),
        ]
    )
    return_index = (
        (own_rows & 255).reshape(12, 1, 512),
        (own_rows >> 8).reshape(12, 1, 512),
    )
    for repeat_at in range(STEPS):
        magnet = path_step(magnet, boundary_matrix, trace_index, return_index)
    return magnet


def solution(mesh):
    return jax.shard_map(
        body,
        mesh=mesh,
        in_specs=(P(None, "cols", "rows", None), P("rows", "cols"), P(), P()),
        out_specs=P(None, "cols", "rows", None),
        check_vma=False,
    )
```

```python
import jax
import jax.numpy as jnp
from jax import lax
from jax.experimental import pallas as pl
from jax.experimental.pallas import tpu as pltpu
from jax.sharding import PartitionSpec as P

GRID = 64
STEPS = 2
ROWS = 8
COLS = 16
NB = 24576
PLANES = 8
PLANE = GRID * GRID
COL_BLOCK = NB // COLS
CHUNKS = NB // ROWS // 256
OWN = 4
SEEN = 6
PIECE = 256
WIDE = 1024
F32 = jnp.float32
BF16 = jnp.bfloat16
PART = F32
POT = BF16

exchange_coef = 0.25
demag_coef = 2.0
time_step = 0.2
spring_coef = 2.0
entries = 3.0 * GRID * GRID * GRID


def lanes_of(width):
    return lax.broadcasted_iota(jnp.int32, (8, width), 1)


def neighbours_y(values, before, after):
    width = values.shape[1]
    whole = jnp.concatenate([before, values, after], axis=1)
    pieces = [pltpu.roll(whole[:, 128 * k : 128 * k + 128], 64, 1) for k in range(width // 128 + 2)]
    low = lanes_of(128) < 64
    north = [jnp.where(low, pieces[k + 1], pieces[k + 2]) for k in range(width // 128)]
    south = [jnp.where(low, pieces[k], pieces[k + 1]) for k in range(width // 128)]
    return jnp.concatenate(north, axis=1), jnp.concatenate(south, axis=1)


def neighbours_x(values):
    pieces = [values[:, 128 * k : 128 * k + 128] for k in range(values.shape[1] // 128)]
    east = jnp.concatenate([pltpu.roll(piece, 127, 1) for piece in pieces], axis=1)
    west = jnp.concatenate([pltpu.roll(piece, 1, 1) for piece in pieces], axis=1)
    return east, west


def neighbours_z(values, below, above):
    width = values.shape[1]
    plane = lax.broadcasted_iota(jnp.int32, (8, width), 0)
    upper = jnp.where(plane == 7, jnp.broadcast_to(above, (8, width)), pltpu.roll(values, 7, 0))
    lower = jnp.where(plane == 0, jnp.broadcast_to(below, (8, width)), pltpu.roll(values, 1, 0))
    return upper, lower


def sides(read, chunk):
    start = WIDE * chunk
    centre = read(start, WIDE)
    before = read(start - 128, 128) if chunk > 0 else centre[:, :128]
    after = read(start + WIDE, 128) if start + WIDE < PLANE else centre[:, :128]
    return centre, before, after


def first_kernel(magnet_ref, head_ref, tail_ref):
    for c in range(3):
        for p in range(OWN):
            row = c * OWN + p
            head_ref[row : row + 1, :] = magnet_ref[c, p, 0:1, :]
            tail_ref[row : row + 1, :] = magnet_ref[c, p, 7:8, :]


def edge_planes(magnet):
    shape = jax.ShapeDtypeStruct((3 * OWN, PLANE), F32)
    return pl.pallas_call(first_kernel, out_shape=(shape, shape), name="edge_planes")(magnet)


def surface_kernel(at_ref, magnet_ref, below_ref, above_ref, out_ref, left_ref, right_ref, plane_ref):
    rows_at = at_ref[0]
    lane = lanes_of(128)
    half = lane & 63
    for p in range(OWN):
        side_x = jnp.zeros((8, 128), F32)
        side_y = jnp.zeros((8, 128), F32)
        for chunk in range(PLANE // WIDE):
            span = pl.ds(WIDE * chunk, WIDE)
            wide_lane = lanes_of(WIDE)
            x_at = wide_lane & 63
            y_at = (wide_lane + WIDE * chunk) >> 6
            east, west = neighbours_x(magnet_ref[0, p, :, span])
            north, south = neighbours_y(*sides(lambda s, w: magnet_ref[1, p, :, pl.ds(s, w)], chunk))
            row = 2 * OWN + p
            upper, lower = neighbours_z(
                magnet_ref[2, p, :, span], below_ref[row : row + 1, span], above_ref[row : row + 1, span]
            )
            diverge = 0.5 * (
                jnp.where(x_at < GRID - 1, east, 0.0)
                - jnp.where(x_at > 0, west, 0.0)
                + jnp.where(y_at < GRID - 1, north, 0.0)
                - jnp.where(y_at > 0, south, 0.0)
                + upper
                - lower
            )
            chosen = jnp.where(rows_at == 0, diverge[0:1], diverge[7:8])
            for j in range(WIDE // 256):
                at = 16 * p + chunk * (WIDE // 256) + j
                plane_ref[at : at + 1, :] = chosen[:, 256 * j : 256 * j + 256]
            for j in range(WIDE // 128):
                k = chunk * (WIDE // 128) + j
                piece = diverge[:, 128 * j : 128 * j + 128]
                kept = jnp.where(half == 0, piece, 0.0) + jnp.where(
                    half == 32, pltpu.roll(piece, 33, 1), 0.0
                )
                side_x = side_x + (pltpu.roll(kept, k, 1) if k else kept)
            if chunk == 0:
                side_y = diverge[:, :128]
            if chunk == PLANE // WIDE - 1:
                side_y = jnp.where(lane < 64, side_y, diverge[:, WIDE - 128 :])
        cycle = jnp.concatenate([side_y, side_x], axis=1)
        plane_ref[64 + 8 * p : 72 + 8 * p, :] = cycle
    whole = jnp.concatenate([plane_ref[64:96, :], plane_ref[0:64, :]], axis=0).astype(BF16)
    for r in range(ROWS):
        out_ref[r] = whole
    for p, side_ref in ((0, left_ref), (OWN - 1, right_ref)):
        for c in range(3):
            side_ref[8 * c : 8 * c + 8, :] = magnet_ref[c, p]
            row = c * OWN + p
            side_ref[24 + 2 * c : 25 + 2 * c, :] = below_ref[row : row + 1, :]
            side_ref[25 + 2 * c : 26 + 2 * c, :] = above_ref[row : row + 1, :]


def surface_block(at, magnet, below, above):
    side = jax.ShapeDtypeStruct((32, PLANE), F32)
    vmem = pl.BlockSpec(memory_space=pltpu.VMEM)
    return pl.pallas_call(
        surface_kernel,
        in_specs=[pl.BlockSpec(memory_space=pltpu.SMEM), vmem, vmem, vmem],
        out_shape=(jax.ShapeDtypeStruct((ROWS, 96, 256), BF16), side, side),
        scratch_shapes=[pltpu.VMEM((96, 256), F32)],
        name="surface_block",
    )(at, magnet, below, above)


def lane_choice(low):
    lane = lax.broadcasted_iota(jnp.int32, (256, low.shape[1]), 0)
    return jnp.where(lane == low, 1.0, 0.0).astype(BF16)


def trace_kernel(table_ref, low_ref, high_ref, out_ref):
    table = jnp.concatenate(
        [table_ref[slab, 0:32, :] for slab in range(ROWS)]
        + [table_ref[0, 32:96, :], table_ref[ROWS - 1, 32:96, :]],
        axis=0,
    )
    width = 2 * PIECE
    plane = lax.broadcasted_iota(jnp.int32, (8, width), 0)
    for tile in range(COLS // 2):
        low = low_ref[:, width * tile : width * tile + width]
        high = high_ref[:, width * tile : width * tile + width]
        picked = jnp.dot(table, lane_choice(low), preferred_element_type=F32)
        offset = high - plane
        total = [jnp.zeros((8, width), F32) for _ in range(OWN)]
        for slab in range(ROWS):
            mask = offset == 8 * slab
            for p in range(OWN):
                at = 32 * slab + 8 * p
                total[p] = total[p] + jnp.where(mask, picked[at : at + 8], 0.0)
        for end in range(2):
            for part in range(2):
                mask = offset == 64 + 16 * end + 8 * part
                for p in range(OWN):
                    at = 256 + 64 * end + 16 * p + 8 * part
                    total[p] = total[p] + jnp.where(mask, picked[at : at + 8], 0.0)
        rows = [jnp.sum(total[p], axis=0, keepdims=True) for p in range(OWN)]
        found = jnp.concatenate(rows, axis=0).astype(BF16)
        for r in range(ROWS):
            out_ref[COLS * r + 2 * tile] = found[:, :PIECE]
            out_ref[COLS * r + 2 * tile + 1] = found[:, PIECE:]


def take_trace(table, low, high):
    return pl.pallas_call(
        trace_kernel,
        out_shape=jax.ShapeDtypeStruct((ROWS * COLS, OWN, PIECE), BF16),
        name="take_trace",
    )(table, low, high)


def partial_kernel(owned_ref, matrix_ref, out_ref, traced_ref, rows_ref, stage_ref):
    @pl.when(pl.program_id(0) == 0)
    def _():
        for r in range(COL_BLOCK // PIECE):
            for c in range(COLS):
                traced_ref[OWN * c : OWN * c + OWN, PIECE * r : PIECE * r + PIECE] = owned_ref[
                    COLS * r + c
                ].astype(F32)
        rows_ref[0:8, :] = jnp.zeros((8, 256), F32)
        rows_ref[72:80, :] = jnp.zeros((8, 256), F32)

    traced = traced_ref[...].astype(BF16)
    for part in range(4):
        rows_ref[8:72, :] = lax.dot_general(
            traced,
            matrix_ref[256 * part : 256 * part + 256, :],
            (((1,), (1,)), ((), ())),
            preferred_element_type=F32,
        )
        for c in range(COLS):
            first = 7 + OWN * c
            stage_ref[c, part * SEEN : part * SEEN + SEEN, :] = rows_ref[first : first + SEEN, :]
    out_ref[...] = stage_ref[...].astype(out_ref.dtype)


def partial_potential(owned, matrix):
    rows = 4 * SEEN
    return pl.pallas_call(
        partial_kernel,
        grid=(3,),
        in_specs=[
            pl.BlockSpec((ROWS * COLS, OWN, PIECE), lambda i: (0, 0, 0)),
            pl.BlockSpec((1024, COL_BLOCK), lambda i: (i, 0)),
        ],
        out_specs=pl.BlockSpec((COLS, rows, 256), lambda i: (0, i, 0)),
        out_shape=jax.ShapeDtypeStruct((COLS, 3 * rows, 256), PART),
        scratch_shapes=[
            pltpu.VMEM((64, COL_BLOCK), F32),
            pltpu.VMEM((80, 256), F32),
            pltpu.VMEM((COLS, rows, 256), F32),
        ],
        name="partial_potential",
    )(owned, matrix)


def combine_kernel(parts_ref, out_ref, sum_ref):
    total = parts_ref[0].astype(F32)
    for c in range(1, COLS):
        total = total + parts_ref[c].astype(F32)
    sum_ref[0 : CHUNKS * SEEN, :] = total
    sum_ref[CHUNKS * SEEN :, :] = jnp.zeros((8, 256), F32)
    rows = jnp.concatenate([sum_ref[SEEN * h : SEEN * h + 8, :] for h in range(CHUNKS)], axis=0)
    rows = rows.astype(out_ref.dtype)
    for r in range(ROWS):
        out_ref[r] = rows


def combine(parts):
    return pl.pallas_call(
        combine_kernel,
        out_shape=jax.ShapeDtypeStruct((ROWS, 8 * CHUNKS, 256), POT),
        scratch_shapes=[pltpu.VMEM((CHUNKS * SEEN + 8, 256), F32)],
        name="combine",
    )(parts)


def exchange_kernel(at_ref, magnet_ref, below_ref, above_ref, left_ref, right_ref, all_ref, field_ref):
    rows_at = at_ref[0]
    for i in range(SEEN):
        for c in range(3):
            if i == 0 or i == SEEN - 1:
                side = left_ref if i == 0 else right_ref
                read = lambda s, w: side[8 * c : 8 * c + 8, pl.ds(s, w)]
                low_row = lambda span: side[24 + 2 * c : 25 + 2 * c, span]
                high_row = lambda span: side[25 + 2 * c : 26 + 2 * c, span]
            else:
                row = c * OWN + i - 1
                read = lambda s, w: magnet_ref[c, i - 1, :, pl.ds(s, w)]
                low_row = lambda span: below_ref[row : row + 1, span]
                high_row = lambda span: above_ref[row : row + 1, span]
            for chunk in range(PLANE // WIDE):
                span = pl.ds(WIDE * chunk, WIDE)
                wide_lane = lanes_of(WIDE)
                x_at = wide_lane & 63
                y_at = (wide_lane + WIDE * chunk) >> 6
                centre, before, after = sides(read, chunk)
                east, west = neighbours_x(centre)
                north, south = neighbours_y(centre, before, after)
                upper, lower = neighbours_z(
                    centre,
                    jnp.where(rows_at == 0, centre[0:1], low_row(span)),
                    jnp.where(rows_at == ROWS - 1, centre[7:8], high_row(span)),
                )
                total = (
                    jnp.where(x_at < GRID - 1, east, centre)
                    + jnp.where(x_at > 0, west, centre)
                    + jnp.where(y_at < GRID - 1, north, centre)
                    + jnp.where(y_at > 0, south, centre)
                    + upper
                    + lower
                )
                field_ref[i, c, :, span] = exchange_coef * (total - 6.0 * centre)
                all_ref[i, c, :, span] = centre


def exchange_field(at, magnet, below, above, left, right):
    vmem = pl.BlockSpec(memory_space=pltpu.VMEM)
    shape = jax.ShapeDtypeStruct((SEEN, 3, PLANES, PLANE), F32)
    return pl.pallas_call(
        exchange_kernel,
        in_specs=[pl.BlockSpec(memory_space=pltpu.SMEM)] + [vmem] * 5,
        out_shape=(shape, shape),
        name="exchange_field",
    )(at, magnet, below, above, left, right)


def torque_kernel(at_ref, table_ref, low_ref, high_ref, all_ref, field_ref, out_ref, sums_ref, found_ref, cycle_ref, near_ref, far_ref):
    rows_at = at_ref[0]
    table = table_ref[...].reshape(ROWS * 8 * CHUNKS, 256)
    for tile in range(12):
        low = low_ref[:, 512 * tile : 512 * tile + 512]
        high = high_ref[:, 512 * tile : 512 * tile + 512]
        choice = lane_choice(low)
        if POT == BF16:
            picked = jnp.dot(table, choice, preferred_element_type=F32)
        else:
            top = table.astype(BF16)
            rest = (table - top.astype(F32)).astype(BF16)
            picked = jnp.dot(top, choice, preferred_element_type=F32) + jnp.dot(
                rest, choice, preferred_element_type=F32
            )
        high = jnp.broadcast_to(high, (8, 512))
        total = jnp.zeros((8, 512), F32)
        for h in range(ROWS * CHUNKS):
            total = total + jnp.where(high == h, picked[8 * h : 8 * h + 8], 0.0)
        total = demag_coef * total
        if tile < 4:
            for z in range(2):
                for p in range(SEEN):
                    cycle_ref[p, 2 * tile + z : 2 * tile + z + 1, :] = total[
                        p : p + 1, 256 * z : 256 * z + 256
                    ]
        else:
            for p in range(SEEN):
                found_ref[p, :, 512 * (tile - 4) : 512 * (tile - 3)] = total[p : p + 1]
    lane = lanes_of(128)
    half = lane & 63
    plane_at = lax.broadcasted_iota(jnp.int32, (8, 128), 0)
    sign = jnp.where(
        (plane_at == 0) & (rows_at == 0),
        1.0,
        jnp.where((plane_at == 7) & (rows_at == ROWS - 1), -1.0, 0.0),
    )

    def image(i, carry):
        side_y = cycle_ref[i, :, 0:128]
        side_x = cycle_ref[i, :, 128:256]
        near = jnp.zeros((8, 128), F32)
        far = jnp.zeros((8, 128), F32)
        last = jnp.maximum(i - 1, 0)
        second = jnp.maximum(i - 2, 0)
        for k in range(PLANE // 128):
            span = pl.ds(128 * k, 128)
            m = [all_ref[i, c, :, span] for c in range(3)]
            f = [field_ref[i, c, :, span] for c in range(3)]
            rolled = pltpu.roll(side_x, (128 - k) % 128, 1) if k else side_x
            f[0] = (
                f[0]
                + jnp.where(half == 0, rolled, 0.0)
                - jnp.where(half == 63, pltpu.roll(side_x, 95 - k, 1), 0.0)
            )
            if k == 0:
                f[1] = f[1] + jnp.where(lane < 64, side_y, 0.0)
            if k == PLANE // 128 - 1:
                f[1] = f[1] - jnp.where(lane >= 64, side_y, 0.0)
            f[2] = f[2] + sign * found_ref[i, :, span]
            along = m[0] * f[0] + m[1] * f[1] + m[2] * f[2]
            length = m[0] * m[0] + m[1] * m[1] + m[2] * m[2]
            v = [m[c] - time_step * (m[c] * along - f[c] * length) for c in range(3)]
            scale = lax.rsqrt(v[0] * v[0] + v[1] * v[1] + v[2] * v[2])
            for c in range(3):
                t = v[c] * scale
                out_ref[i, c, :, span] = t
                step = t - out_ref[last, c, :, span]
                near = near + step * step
                step = t - out_ref[second, c, :, span]
                far = far + step * step
        near_ref[i] = near
        far_ref[i] = far
        return carry

    lax.fori_loop(0, SEEN, image, 0)
    blank = jnp.zeros((2, 128), F32)
    sums = jnp.concatenate(
        [jnp.sum(near_ref[i], axis=0, keepdims=True) for i in range(SEEN)]
        + [blank]
        + [jnp.sum(far_ref[i], axis=0, keepdims=True) for i in range(SEEN)]
        + [blank],
        axis=0,
    )
    for r in range(ROWS):
        sums_ref[r] = sums


def torque(at, table, low, high, magnets, field):
    vmem = pl.BlockSpec(memory_space=pltpu.VMEM)
    return pl.pallas_call(
        torque_kernel,
        in_specs=[pl.BlockSpec(memory_space=pltpu.SMEM)] + [vmem] * 5,
        out_shape=(
            jax.ShapeDtypeStruct((SEEN, 3, PLANES, PLANE), F32),
            jax.ShapeDtypeStruct((ROWS, 16, 128), F32),
        ),
        scratch_shapes=[
            pltpu.VMEM((SEEN, 1, PLANE), F32),
            pltpu.VMEM((SEEN, 8, 256), F32),
            pltpu.VMEM((SEEN, 8, 128), F32),
            pltpu.VMEM((SEEN, 8, 128), F32),
        ],
        name="torque",
    )(at, table, low, high, magnets, field)


def tension_kernel(at_ref, sums_ref, torqued_ref, out_ref, *edges):
    cols_at = at_ref[1]
    total = sums_ref[0]
    for r in range(1, ROWS):
        total = total + sums_ref[r]
    total = jnp.sum(total, axis=1, keepdims=True)
    root = jnp.sqrt(total * (1.0 / entries) + 1e-06)
    for p in range(OWN):
        j = p + 1
        coefficient = spring_coef * (root[j + 1 : j + 2] - root[j : j + 1])
        scale = jnp.broadcast_to(coefficient / root[9 + j : 10 + j], (8, 128))
        if p == 0:
            free = cols_at > 0
        elif p == OWN - 1:
            free = cols_at < COLS - 1
        else:
            free = None

        def lanes(k, carry):
            span = pl.ds(pl.multiple_of(128 * k, 128), 128)
            t = [torqued_ref[j, c, :, span] for c in range(3)]
            force = [
                (torqued_ref[j + 1, c, :, span] - torqued_ref[j - 1, c, :, span]) * scale
                for c in range(3)
            ]
            along = force[0] * t[0] + force[1] * t[1] + force[2] * t[2]
            w = [t[c] + force[c] - along * t[c] for c in range(3)]
            size = lax.rsqrt(w[0] * w[0] + w[1] * w[1] + w[2] * w[2])
            for c in range(3):
                new = w[c] * size
                if free is not None:
                    new = jnp.where(free, new, t[c])
                out_ref[c, p, :, span] = new
                if edges:
                    row = c * OWN + p
                    edges[0][row : row + 1, span] = new[0:1]
                    edges[1][row : row + 1, span] = new[7:8]
            return carry

        lax.fori_loop(0, PLANE // 128, lanes, 0, unroll=4)


def tension(at, sums, torqued, with_edges):
    vmem = pl.BlockSpec(memory_space=pltpu.VMEM)
    edge = jax.ShapeDtypeStruct((3 * OWN, PLANE), F32)
    return pl.pallas_call(
        tension_kernel,
        in_specs=[pl.BlockSpec(memory_space=pltpu.SMEM), vmem, vmem],
        out_shape=(jax.ShapeDtypeStruct((3, OWN, PLANES, PLANE), F32),)
        + ((edge, edge) if with_edges else ()),
        name="tension",
    )(at, sums, torqued)


def swap(values, axis):
    return lax.all_to_all(values, axis, split_axis=0, concat_axis=0, tiled=True)


def up(values, axis):
    return lax.ppermute(values, axis, [(i, i + 1) for i in range(lax.axis_size(axis) - 1)])


def down(values, axis):
    return lax.ppermute(values, axis, [(i + 1, i) for i in range(lax.axis_size(axis) - 1)])


def trace_positions(trace_slot, rows_at):
    piece = jnp.minimum(rows_at, COL_BLOCK // PIECE - 1)
    mine = lax.dynamic_slice(
        trace_slot.reshape(COLS, COL_BLOCK), (0, piece * PIECE), (COLS, PIECE)
    )
    high = mine >> 8
    low = mine & 255
    k = (low & 63) >> 1
    odd = low & 1
    far = (low >> 6) & 1
    lane = k + jnp.where(far == 0, odd * 64, 96 - odd * 64)
    low = jnp.where((high < GRID) & (low >= 128), 128 + lane, low)
    return low.reshape(1, COLS * PIECE), high.reshape(1, COLS * PIECE)


def return_positions(return_row, rows_at):
    cycles = lax.dynamic_slice_in_dim(return_row, rows_at * PLANES * 256, PLANES * 256)
    plane = jnp.where(rows_at == 0, return_row[16384:20480], return_row[20480:])
    both = jnp.stack([cycles & 255, cycles >> 8]).reshape(2 * PLANES, 256)
    place = jnp.arange(128, dtype=jnp.int32)
    k = place & 31
    source = jnp.where(
        place < 32, 2 * k, jnp.where(place < 64, 65 + 2 * k, jnp.where(place < 96, 2 * k + 1, 64 + 2 * k))
    )
    order = (source[None, :] == place[:, None]).astype(BF16)
    turned = jnp.dot(both[:, 128:].astype(BF16), order, preferred_element_type=F32).astype(jnp.int32)
    both = jnp.concatenate([both[:, :128], turned], axis=1).reshape(2, PLANES * 256)
    low = jnp.concatenate([both[0], plane & 255])
    high = jnp.concatenate([both[1], plane >> 8])
    return low.reshape(1, -1), high.reshape(1, -1)


def body(m_start, boundary_matrix, trace_slot, return_row):
    rows_at = lax.axis_index("rows")
    cols_at = lax.axis_index("cols")
    at = jnp.stack([rows_at, cols_at]).astype(jnp.int32)
    trace_at = trace_positions(trace_slot, rows_at)
    return_at = return_positions(return_row, rows_at)
    magnet = m_start
    head, tail = edge_planes(magnet)
    for repeat_at in range(STEPS):
        below = up(tail, "rows")
        above = down(head, "rows")
        block, left, right = surface_block(at, magnet, below, above)
        table = swap(block, "rows")
        from_left = up(right, "cols")
        from_right = down(left, "cols")
        traced = take_trace(table, *trace_at)
        owned = swap(traced, ("rows", "cols"))
        magnets, field = exchange_field(at, magnet, below, above, from_left, from_right)
        parts = swap(partial_potential(owned, boundary_matrix), "cols")
        potential = swap(combine(parts), "rows")
        torqued, sums = torque(at, potential, *return_at, magnets, field)
        sums = swap(sums, "rows")
        more = repeat_at + 1 < STEPS
        made = tension(at, sums, torqued, more)
        magnet = made[0]
        if more:
            head, tail = made[1:]
    return magnet


def solution(mesh):
    return jax.shard_map(
        body,
        mesh=mesh,
        in_specs=(P(None, "cols", "rows", None), P("rows", "cols"), P(), P()),
        out_specs=P(None, "cols", "rows", None),
        check_vma=False,
    )
```

```python
import jax
import jax.numpy as jnp
from jax import lax
from jax.experimental import pallas as pl
from jax.experimental.pallas import tpu as pltpu
from jax.sharding import PartitionSpec as P

GRID = 64
STEPS = 2
ROWS = 8
COLS = 16
NB = 24576
PLANES = 8
PLANE = GRID * GRID
COL_BLOCK = NB // COLS
CHUNKS = NB // ROWS // 256
OWN = 4
BLOCK = 144
SEEN = 6
PIECE = 256
WIDE = 1024
F32 = jnp.float32
BF16 = jnp.bfloat16
PART = F32
POT = BF16
EXCHANGE_MIB = 60

exchange_coef = 0.25
demag_coef = 2.0
time_step = 0.2
spring_coef = 2.0
entries = 3.0 * GRID * GRID * GRID


def lanes_of(width):
    return lax.broadcasted_iota(jnp.int32, (8, width), 1)


def neighbours_y(values, before, after):
    width = values.shape[1]
    whole = jnp.concatenate([before, values, after], axis=1)
    pieces = [pltpu.roll(whole[:, 128 * k : 128 * k + 128], 64, 1) for k in range(width // 128 + 2)]
    low = lanes_of(128) < 64
    north = [jnp.where(low, pieces[k + 1], pieces[k + 2]) for k in range(width // 128)]
    south = [jnp.where(low, pieces[k], pieces[k + 1]) for k in range(width // 128)]
    return jnp.concatenate(north, axis=1), jnp.concatenate(south, axis=1)


def neighbours_x(values):
    pieces = [values[:, 128 * k : 128 * k + 128] for k in range(values.shape[1] // 128)]
    east = jnp.concatenate([pltpu.roll(piece, 127, 1) for piece in pieces], axis=1)
    west = jnp.concatenate([pltpu.roll(piece, 1, 1) for piece in pieces], axis=1)
    return east, west


def neighbours_z(values, below, above):
    width = values.shape[1]
    plane = lax.broadcasted_iota(jnp.int32, (8, width), 0)
    upper = jnp.where(plane == 7, jnp.broadcast_to(above, (8, width)), pltpu.roll(values, 7, 0))
    lower = jnp.where(plane == 0, jnp.broadcast_to(below, (8, width)), pltpu.roll(values, 1, 0))
    return upper, lower


def sides(read, chunk):
    start = WIDE * chunk
    centre = read(start, WIDE)
    before = read(start - 128, 128) if chunk > 0 else centre[:, :128]
    after = read(start + WIDE, 128) if start + WIDE < PLANE else centre[:, :128]
    return centre, before, after


def planes_kernel(magnet_ref, left_ref, right_ref, head_ref, tail_ref):
    for c in range(3):
        for i in range(SEEN):
            row = i
            if i == 0:
                source = left_ref.at[c]
            elif i == SEEN - 1:
                source = right_ref.at[c]
            else:
                source = magnet_ref.at[c, i - 1]
            head_ref[row, c : c + 1, :] = source[0:1, :]
            tail_ref[row, c : c + 1, :] = source[7:8, :]


def edge_planes(magnet, left, right):
    shape = jax.ShapeDtypeStruct((SEEN, 3, PLANE), F32)
    return pl.pallas_call(
        planes_kernel,
        out_shape=(shape, shape),
        name="edge_planes",
        compiler_params=pltpu.CompilerParams(vmem_limit_bytes=6 << 20),
    )(magnet, left, right)


def three_parts(values):
    top = values.astype(BF16).astype(F32)
    rest = values - top
    middle = rest.astype(BF16).astype(F32)
    return top, middle, rest - middle


def gather_sides(total_x, piece, k, half):
    kept = jnp.where(half == 0, piece, 0.0) + jnp.where(half == 32, pltpu.roll(piece, 33, 1), 0.0)
    return total_x + (pltpu.roll(kept, k, 1) if k else kept)


def write_block(rows_at, magnet_ref, out_ref, stage_ref):
    lane = lanes_of(128)
    half = lane & 63
    for p in range(OWN):
        side_x = jnp.zeros((8, 128), F32)
        side_y = jnp.zeros((8, 128), F32)
        spin_x = jnp.zeros((8, 128), F32)
        spin_y = jnp.zeros((8, 128), F32)
        for chunk in range(PLANE // WIDE):
            span = pl.ds(WIDE * chunk, WIDE)
            wide_lane = lanes_of(WIDE)
            x_at = wide_lane & 63
            y_at = (wide_lane + WIDE * chunk) >> 6
            east, west = neighbours_x(magnet_ref[0, p, :, span])
            north, south = neighbours_y(*sides(lambda s, w: magnet_ref[1, p, :, pl.ds(s, w)], chunk))
            spin = magnet_ref[2, p, :, span]
            nothing = jnp.zeros((1, WIDE), F32)
            upper, lower = neighbours_z(spin, nothing, nothing)
            diverge = 0.5 * (
                jnp.where(x_at < GRID - 1, east, 0.0)
                - jnp.where(x_at > 0, west, 0.0)
                + jnp.where(y_at < GRID - 1, north, 0.0)
                - jnp.where(y_at > 0, south, 0.0)
                + upper
                - lower
            )
            chosen = jnp.where(rows_at == 0, diverge[0:1], diverge[7:8])
            for j in range(WIDE // 256):
                at = 32 + 4 * (chunk * (WIDE // 256) + j) + p
                stage_ref[at : at + 1, :] = chosen[:, 256 * j : 256 * j + 256]
            for j in range(WIDE // 128):
                k = chunk * (WIDE // 128) + j
                side_x = gather_sides(side_x, diverge[:, 128 * j : 128 * j + 128], k, half)
                spin_x = gather_sides(spin_x, spin[:, 128 * j : 128 * j + 128], k, half)
            if chunk == 0:
                side_y = diverge[:, :128]
                spin_y = spin[:, :128]
            if chunk == PLANE // WIDE - 1:
                side_y = jnp.where(lane < 64, side_y, diverge[:, WIDE - 128 :])
                spin_y = jnp.where(lane < 64, spin_y, spin[:, WIDE - 128 :])
        cycle = jnp.concatenate([side_y, side_x], axis=1)
        for z in range(PLANES):
            stage_ref[4 * z + p : 4 * z + p + 1, :] = cycle[z : z + 1]
        parts = three_parts(cycle) + three_parts(jnp.concatenate([spin_y, spin_x], axis=1))
        for n in range(6):
            for end in range(2):
                at = 96 + 24 * end + 4 * n + p
                stage_ref[at : at + 1, :] = parts[n][7 * end : 7 * end + 1]
    whole = stage_ref[...].astype(BF16)
    for r in range(ROWS):
        out_ref[r] = whole


def surface_kernel(at_ref, magnet_ref, out_ref, stage_ref):
    write_block(at_ref[0], magnet_ref, out_ref, stage_ref)


def surface_block(at, magnet):
    return pl.pallas_call(
        surface_kernel,
        in_specs=[pl.BlockSpec(memory_space=pltpu.SMEM), pl.BlockSpec(memory_space=pltpu.VMEM)],
        out_shape=jax.ShapeDtypeStruct((ROWS, BLOCK, 256), BF16),
        scratch_shapes=[pltpu.VMEM((BLOCK, 256), F32)],
        name="surface_block",
        compiler_params=pltpu.CompilerParams(vmem_limit_bytes=8 << 20),
    )(at, magnet)


def lane_choice(low):
    lane = lax.broadcasted_iota(jnp.int32, (256, low.shape[1]), 0)
    return jnp.where(lane == low, 1.0, 0.0).astype(BF16)


def trace_kernel(table_ref, low_ref, high_ref, out_ref, whole_ref):
    ends = [table_ref[slab, 96:BLOCK, :].astype(F32) for slab in range(ROWS)]

    def joined(slab, end, first):
        at = 24 * end + 4 * first
        part = ends[slab]
        return part[at : at + 4] + (part[at + 4 : at + 8] + part[at + 8 : at + 12])

    for slab in range(ROWS):
        base = 32 * slab
        whole_ref[base : base + 32, :] = table_ref[slab, 0:32, :].astype(F32)
        if slab > 0:
            whole_ref[base : base + 4, :] = joined(slab, 0, 0) - 0.5 * joined(slab - 1, 1, 3)
        if slab < ROWS - 1:
            whole_ref[base + 28 : base + 32, :] = joined(slab, 1, 0) + 0.5 * joined(slab + 1, 0, 3)
    whole_ref[256:320, :] = table_ref[0, 32:96, :].astype(F32)
    whole_ref[320:384, :] = table_ref[ROWS - 1, 32:96, :].astype(F32)
    table = whole_ref[...].astype(BF16)
    width = 2 * PIECE
    for tile in range(COLS // 2):
        low = low_ref[:, width * tile : width * tile + width]
        high = high_ref[:, width * tile : width * tile + width]
        picked = jnp.dot(table, lane_choice(low), preferred_element_type=F32)
        offset = high - (lax.broadcasted_iota(jnp.int32, (8, width), 0) >> 2)
        total = jnp.zeros((8, width), F32)
        for pair in range(48):
            total = total + jnp.where(offset == 2 * pair, picked[8 * pair : 8 * pair + 8], 0.0)
        found = (total[0:4] + total[4:8]).astype(BF16)
        for r in range(ROWS):
            out_ref[COLS * r + 2 * tile] = found[:, :PIECE]
            out_ref[COLS * r + 2 * tile + 1] = found[:, PIECE:]


def take_trace(table, low, high):
    return pl.pallas_call(
        trace_kernel,
        out_shape=jax.ShapeDtypeStruct((ROWS * COLS, OWN, PIECE), BF16),
        scratch_shapes=[pltpu.VMEM((384, 256), F32)],
        name="take_trace",
        compiler_params=pltpu.CompilerParams(vmem_limit_bytes=12 << 20),
    )(table, low, high)


def partial_kernel(owned_ref, matrix_ref, out_ref, traced_ref, rows_ref, stage_ref):
    @pl.when(pl.program_id(0) == 0)
    def _():
        for r in range(COL_BLOCK // PIECE):
            for c in range(COLS):
                traced_ref[OWN * c : OWN * c + OWN, PIECE * r : PIECE * r + PIECE] = owned_ref[
                    COLS * r + c
                ].astype(F32)
        rows_ref[0:8, :] = jnp.zeros((8, 256), F32)
        rows_ref[72:80, :] = jnp.zeros((8, 256), F32)

    traced = traced_ref[...].astype(BF16)
    for part in range(4):
        rows_ref[8:72, :] = lax.dot_general(
            traced,
            matrix_ref[256 * part : 256 * part + 256, :],
            (((1,), (1,)), ((), ())),
            preferred_element_type=F32,
        )
        for c in range(COLS):
            first = 7 + OWN * c
            stage_ref[c, part * SEEN : part * SEEN + SEEN, :] = rows_ref[first : first + SEEN, :]
    out_ref[...] = stage_ref[...].astype(out_ref.dtype)


def partial_potential(owned, matrix):
    rows = 4 * SEEN
    return pl.pallas_call(
        partial_kernel,
        grid=(3,),
        in_specs=[
            pl.BlockSpec((ROWS * COLS, OWN, PIECE), lambda i: (0, 0, 0)),
            pl.BlockSpec((1024, COL_BLOCK), lambda i: (i, 0)),
        ],
        out_specs=pl.BlockSpec((COLS, rows, 256), lambda i: (0, i, 0)),
        out_shape=jax.ShapeDtypeStruct((COLS, 3 * rows, 256), PART),
        scratch_shapes=[
            pltpu.VMEM((64, COL_BLOCK), F32),
            pltpu.VMEM((80, 256), F32),
            pltpu.VMEM((COLS, rows, 256), F32),
        ],
        name="partial_potential",
        compiler_params=pltpu.CompilerParams(vmem_limit_bytes=55 << 20),
    )(owned, matrix)


def combine_kernel(parts_ref, out_ref, sum_ref):
    total = parts_ref[0].astype(F32)
    for c in range(1, COLS):
        total = total + parts_ref[c].astype(F32)
    sum_ref[0 : CHUNKS * SEEN, :] = total
    sum_ref[CHUNKS * SEEN :, :] = jnp.zeros((8, 256), F32)
    rows = jnp.concatenate([sum_ref[SEEN * h : SEEN * h + 8, :] for h in range(CHUNKS)], axis=0)
    rows = rows.astype(out_ref.dtype)
    for r in range(ROWS):
        out_ref[r] = rows


def combine(parts):
    return pl.pallas_call(
        combine_kernel,
        out_shape=jax.ShapeDtypeStruct((ROWS, 8 * CHUNKS, 256), POT),
        scratch_shapes=[pltpu.VMEM((CHUNKS * SEEN + 8, 256), F32)],
        name="combine",
        compiler_params=pltpu.CompilerParams(vmem_limit_bytes=6 << 20),
    )(parts)


def laplace_of(rows_at, read, low_row, high_row, write):
    for chunk in range(PLANE // WIDE):
        span = pl.ds(WIDE * chunk, WIDE)
        wide_lane = lanes_of(WIDE)
        x_at = wide_lane & 63
        y_at = (wide_lane + WIDE * chunk) >> 6
        centre, before, after = sides(read, chunk)
        east, west = neighbours_x(centre)
        north, south = neighbours_y(centre, before, after)
        upper, lower = neighbours_z(
            centre,
            jnp.where(rows_at == 0, centre[0:1], low_row(span)),
            jnp.where(rows_at == ROWS - 1, centre[7:8], high_row(span)),
        )
        total = (
            jnp.where(x_at < GRID - 1, east, centre)
            + jnp.where(x_at > 0, west, centre)
            + jnp.where(y_at < GRID - 1, north, centre)
            + jnp.where(y_at > 0, south, centre)
            + upper
            + lower
        )
        write(span, centre, exchange_coef * (total - 6.0 * centre))


def exchange_kernel(at_ref, magnet_ref, below_ref, above_ref, left_ref, right_ref, all_ref, field_ref):
    rows_at = at_ref[0]
    i = pl.program_id(0)

    def one(source, c):
        def write(span, centre, value):
            all_ref[0, c, :, span] = centre
            field_ref[0, c, :, span] = value

        laplace_of(
            rows_at,
            lambda s, w: source[:, pl.ds(s, w)],
            lambda span: below_ref[0, c : c + 1, span],
            lambda span: above_ref[0, c : c + 1, span],
            write,
        )

    @pl.when(i == 0)
    def _():
        for c in range(3):
            one(left_ref.at[c], c)

    @pl.when((i > 0) & (i < SEEN - 1))
    def _():
        for c in range(3):
            one(magnet_ref.at[c, 0], c)

    @pl.when(i == SEEN - 1)
    def _():
        for c in range(3):
            one(right_ref.at[c], c)


def exchange_field(at, magnet, below, above, left, right):
    shape = jax.ShapeDtypeStruct((SEEN, 3, PLANES, PLANE), F32)
    block = pl.BlockSpec((1, 3, PLANES, PLANE), lambda i: (i, 0, 0, 0))
    rows = pl.BlockSpec((1, 3, PLANE), lambda i: (i, 0, 0))
    whole = pl.BlockSpec((3, PLANES, PLANE), lambda i: (0, 0, 0))
    own = pl.BlockSpec((3, 1, PLANES, PLANE), lambda i: (0, jnp.clip(i - 1, 0, OWN - 1), 0, 0))
    return pl.pallas_call(
        exchange_kernel,
        grid=(SEEN,),
        in_specs=[pl.BlockSpec(memory_space=pltpu.SMEM), own, rows, rows, whole, whole],
        out_specs=(block, block),
        out_shape=(shape, shape),
        name="exchange_field",
        compiler_params=pltpu.CompilerParams(vmem_limit_bytes=EXCHANGE_MIB << 20),
    )(at, magnet, below, above, left, right)


def find_returned(table_ref, low_ref, high_ref, found_ref, cycle_ref):
    table = table_ref[...].reshape(ROWS * 8 * CHUNKS, 256)
    for tile in range(12):
        low = low_ref[:, 512 * tile : 512 * tile + 512]
        high = high_ref[:, 512 * tile : 512 * tile + 512]
        choice = lane_choice(low)
        if POT == BF16:
            picked = jnp.dot(table, choice, preferred_element_type=F32)
        else:
            top = table.astype(BF16)
            rest = (table - top.astype(F32)).astype(BF16)
            picked = jnp.dot(top, choice, preferred_element_type=F32) + jnp.dot(
                rest, choice, preferred_element_type=F32
            )
        high = jnp.broadcast_to(high, (8, 512))
        total = jnp.zeros((8, 512), F32)
        for h in range(ROWS * CHUNKS):
            total = total + jnp.where(high == h, picked[8 * h : 8 * h + 8], 0.0)
        total = demag_coef * total
        if tile < 4:
            for z in range(2):
                for p in range(SEEN):
                    cycle_ref[p, 2 * tile + z : 2 * tile + z + 1, :] = total[
                        p : p + 1, 256 * z : 256 * z + 256
                    ]
        else:
            for p in range(SEEN):
                found_ref[p, :, 512 * (tile - 4) : 512 * (tile - 3)] = total[p : p + 1]


def torque_kernel(at_ref, table_ref, low_ref, high_ref, all_ref, field_ref, out_ref, sums_ref, found_ref, cycle_ref, near_ref, far_ref):
    rows_at = at_ref[0]
    i = pl.program_id(0)

    @pl.when(i == 0)
    def _():
        find_returned(table_ref, low_ref, high_ref, found_ref, cycle_ref)

    lane = lanes_of(128)
    half = lane & 63
    plane_at = lax.broadcasted_iota(jnp.int32, (8, 128), 0)
    sign = jnp.where(
        (plane_at == 0) & (rows_at == 0),
        1.0,
        jnp.where((plane_at == 7) & (rows_at == ROWS - 1), -1.0, 0.0),
    )

    side_y = cycle_ref[i, :, 0:128]
    side_x = cycle_ref[i, :, 128:256]
    near = jnp.zeros((8, 128), F32)
    far = jnp.zeros((8, 128), F32)
    last = jnp.maximum(i - 1, 0)
    second = jnp.maximum(i - 2, 0)
    for k in range(PLANE // 128):
        span = pl.ds(128 * k, 128)
        m = [all_ref[0, c, :, span] for c in range(3)]
        f = [field_ref[0, c, :, span] for c in range(3)]
        rolled = pltpu.roll(side_x, (128 - k) % 128, 1) if k else side_x
        f[0] = (
            f[0]
            + jnp.where(half == 0, rolled, 0.0)
            - jnp.where(half == 63, pltpu.roll(side_x, 95 - k, 1), 0.0)
        )
        if k == 0:
            f[1] = f[1] + jnp.where(lane < 64, side_y, 0.0)
        if k == PLANE // 128 - 1:
            f[1] = f[1] - jnp.where(lane >= 64, side_y, 0.0)
        f[2] = f[2] + sign * found_ref[i, :, span]
        along = m[0] * f[0] + m[1] * f[1] + m[2] * f[2]
        length = m[0] * m[0] + m[1] * m[1] + m[2] * m[2]
        v = [m[c] - time_step * (m[c] * along - f[c] * length) for c in range(3)]
        scale = lax.rsqrt(v[0] * v[0] + v[1] * v[1] + v[2] * v[2])
        for c in range(3):
            t = v[c] * scale
            out_ref[i, c, :, span] = t
            step = t - out_ref[last, c, :, span]
            near = near + step * step
            step = t - out_ref[second, c, :, span]
            far = far + step * step
    near_ref[i] = near
    far_ref[i] = far

    @pl.when(i == SEEN - 1)
    def _():
        blank = jnp.zeros((2, 128), F32)
        sums = jnp.concatenate(
            [jnp.sum(near_ref[n], axis=0, keepdims=True) for n in range(SEEN)]
            + [blank]
            + [jnp.sum(far_ref[n], axis=0, keepdims=True) for n in range(SEEN)]
            + [blank],
            axis=0,
        )
        for r in range(ROWS):
            sums_ref[r] = sums


def torque(at, table, low, high, magnets, field):
    vmem = pl.BlockSpec(memory_space=pltpu.VMEM)
    block = pl.BlockSpec((1, 3, PLANES, PLANE), lambda i: (i, 0, 0, 0))
    return pl.pallas_call(
        torque_kernel,
        grid=(SEEN,),
        in_specs=[pl.BlockSpec(memory_space=pltpu.SMEM), vmem, vmem, vmem, block, block],
        out_specs=(vmem, vmem),
        out_shape=(
            jax.ShapeDtypeStruct((SEEN, 3, PLANES, PLANE), F32),
            jax.ShapeDtypeStruct((ROWS, 16, 128), F32),
        ),
        scratch_shapes=[
            pltpu.VMEM((SEEN, 1, PLANE), F32),
            pltpu.VMEM((SEEN, 8, 256), F32),
            pltpu.VMEM((SEEN, 8, 128), F32),
            pltpu.VMEM((SEEN, 8, 128), F32),
        ],
        name="torque",
        compiler_params=pltpu.CompilerParams(vmem_limit_bytes=20 << 20),
    )(at, table, low, high, magnets, field)


def tension_kernel(at_ref, sums_ref, torqued_ref, out_ref, *more):
    cols_at = at_ref[1]
    total = sums_ref[0]
    for r in range(1, ROWS):
        total = total + sums_ref[r]
    total = jnp.sum(total, axis=1, keepdims=True)
    root = jnp.sqrt(total * (1.0 / entries) + 1e-06)
    for p in range(OWN):
        j = p + 1
        coefficient = spring_coef * (root[j + 1 : j + 2] - root[j : j + 1])
        scale = jnp.broadcast_to(coefficient / root[9 + j : 10 + j], (8, 128))
        if p == 0:
            free = cols_at > 0
        elif p == OWN - 1:
            free = cols_at < COLS - 1
        else:
            free = None

        def lanes(k, carry):
            span = pl.ds(pl.multiple_of(128 * k, 128), 128)
            t = [torqued_ref[j, c, :, span] for c in range(3)]
            force = [
                (torqued_ref[j + 1, c, :, span] - torqued_ref[j - 1, c, :, span]) * scale
                for c in range(3)
            ]
            along = force[0] * t[0] + force[1] * t[1] + force[2] * t[2]
            w = [t[c] + force[c] - along * t[c] for c in range(3)]
            size = lax.rsqrt(w[0] * w[0] + w[1] * w[1] + w[2] * w[2])
            for c in range(3):
                new = w[c] * size
                if free is not None:
                    new = jnp.where(free, new, t[c])
                out_ref[c, p, :, span] = new
            return carry

        lax.fori_loop(0, PLANE // 128, lanes, 0, unroll=4)
    if more:
        write_block(at_ref[0], out_ref, *more)


def tension(at, sums, torqued, with_block):
    vmem = pl.BlockSpec(memory_space=pltpu.VMEM)
    block = jax.ShapeDtypeStruct((ROWS, BLOCK, 256), BF16)
    return pl.pallas_call(
        tension_kernel,
        in_specs=[pl.BlockSpec(memory_space=pltpu.SMEM), vmem, vmem],
        out_shape=(jax.ShapeDtypeStruct((3, OWN, PLANES, PLANE), F32),) + ((block,) if with_block else ()),
        scratch_shapes=[pltpu.VMEM((BLOCK, 256), F32)] if with_block else [],
        name="tension",
        compiler_params=pltpu.CompilerParams(vmem_limit_bytes=10 << 20),
    )(at, sums, torqued)


def swap(values, axis):
    return lax.all_to_all(values, axis, split_axis=0, concat_axis=0, tiled=True)


def up(values, axis):
    return lax.ppermute(values, axis, [(i, i + 1) for i in range(lax.axis_size(axis) - 1)])


def down(values, axis):
    return lax.ppermute(values, axis, [(i + 1, i) for i in range(lax.axis_size(axis) - 1)])


def trace_positions(trace_slot, rows_at):
    piece = jnp.minimum(rows_at, COL_BLOCK // PIECE - 1)
    mine = lax.dynamic_slice(
        trace_slot.reshape(COLS, COL_BLOCK), (0, piece * PIECE), (COLS, PIECE)
    )
    high = mine >> 8
    low = mine & 255
    k = (low & 63) >> 1
    odd = low & 1
    far = (low >> 6) & 1
    lane = k + jnp.where(far == 0, odd * 64, 96 - odd * 64)
    low = jnp.where((high < GRID) & (low >= 128), 128 + lane, low)
    return low.reshape(1, COLS * PIECE), high.reshape(1, COLS * PIECE)


def return_positions(return_row, rows_at):
    cycles = lax.dynamic_slice_in_dim(return_row, rows_at * PLANES * 256, PLANES * 256)
    plane = jnp.where(rows_at == 0, return_row[16384:20480], return_row[20480:])
    both = jnp.stack([cycles & 255, cycles >> 8]).reshape(2 * PLANES, 256)
    place = jnp.arange(128, dtype=jnp.int32)
    k = place & 31
    source = jnp.where(
        place < 32, 2 * k, jnp.where(place < 64, 65 + 2 * k, jnp.where(place < 96, 2 * k + 1, 64 + 2 * k))
    )
    order = (source[None, :] == place[:, None]).astype(BF16)
    turned = jnp.dot(both[:, 128:].astype(BF16), order, preferred_element_type=F32).astype(jnp.int32)
    both = jnp.concatenate([both[:, :128], turned], axis=1).reshape(2, PLANES * 256)
    low = jnp.concatenate([both[0], plane & 255])
    high = jnp.concatenate([both[1], plane >> 8])
    return low.reshape(1, -1), high.reshape(1, -1)


def body(m_start, boundary_matrix, trace_slot, return_row):
    rows_at = lax.axis_index("rows")
    cols_at = lax.axis_index("cols")
    at = jnp.stack([rows_at, cols_at]).astype(jnp.int32)
    trace_at = trace_positions(trace_slot, rows_at)
    return_at = return_positions(return_row, rows_at)
    magnet = m_start
    block = surface_block(at, magnet)
    for repeat_at in range(STEPS):
        table = swap(block, "rows")
        from_left = up(magnet[:, OWN - 1], "cols")
        from_right = down(magnet[:, 0], "cols")
        traced = take_trace(table, *trace_at)
        owned = swap(traced, ("rows", "cols"))
        owned, from_left, from_right = lax.optimization_barrier((owned, from_left, from_right))
        head, tail = edge_planes(magnet, from_left, from_right)
        parts = swap(partial_potential(owned, boundary_matrix), "cols")
        below = up(tail, "rows")
        above = down(head, "rows")
        parts, below, above = lax.optimization_barrier((parts, below, above))
        potential = swap(combine(parts), "rows")
        magnets, field = exchange_field(at, magnet, below, above, from_left, from_right)
        torqued, sums = torque(at, potential, *return_at, magnets, field)
        sums = swap(sums, "rows")
        made = tension(at, sums, torqued, repeat_at + 1 < STEPS)
        magnet = made[0]
        block = made[-1]
    return magnet


def solution(mesh):
    return jax.shard_map(
        body,
        mesh=mesh,
        in_specs=(P(None, "cols", "rows", None), P("rows", "cols"), P(), P()),
        out_specs=P(None, "cols", "rows", None),
        check_vma=False,
    )
```

```python
import jax
import jax.numpy as jnp
from jax import lax
from jax.experimental import pallas as pl
from jax.experimental.pallas import tpu as pltpu
from jax.sharding import PartitionSpec as P

GRID = 64
STEPS = 2
ROWS = 8
COLS = 16
NB = 24576
PLANES = 8
PLANE = GRID * GRID
COL_BLOCK = NB // COLS
CHUNKS = NB // ROWS // 256
OWN = 4
BLOCK = 144
SEEN = 6
PIECE = 256
WIDE = 1024
F32 = jnp.float32
BF16 = jnp.bfloat16
PART = F32
POT = BF16
TOGETHER = 4

exchange_coef = 0.25
demag_coef = 2.0
time_step = 0.2
spring_coef = 2.0
entries = 3.0 * GRID * GRID * GRID


def lanes_of(width):
    return lax.broadcasted_iota(jnp.int32, (8, width), 1)


def neighbours_y(values, before, after):
    width = values.shape[1]
    whole = jnp.concatenate([before, values, after], axis=1)
    pieces = [pltpu.roll(whole[:, 128 * k : 128 * k + 128], 64, 1) for k in range(width // 128 + 2)]
    low = lanes_of(128) < 64
    north = [jnp.where(low, pieces[k + 1], pieces[k + 2]) for k in range(width // 128)]
    south = [jnp.where(low, pieces[k], pieces[k + 1]) for k in range(width // 128)]
    return jnp.concatenate(north, axis=1), jnp.concatenate(south, axis=1)


def neighbours_x(values):
    pieces = [values[:, 128 * k : 128 * k + 128] for k in range(values.shape[1] // 128)]
    east = jnp.concatenate([pltpu.roll(piece, 127, 1) for piece in pieces], axis=1)
    west = jnp.concatenate([pltpu.roll(piece, 1, 1) for piece in pieces], axis=1)
    return east, west


def neighbours_z(values, below, above):
    width = values.shape[1]
    plane = lax.broadcasted_iota(jnp.int32, (8, width), 0)
    upper = jnp.where(plane == 7, jnp.broadcast_to(above, (8, width)), pltpu.roll(values, 7, 0))
    lower = jnp.where(plane == 0, jnp.broadcast_to(below, (8, width)), pltpu.roll(values, 1, 0))
    return upper, lower


def sides(read, chunk):
    start = WIDE * chunk
    centre = read(start, WIDE)
    before = read(start - 128, 128) if chunk > 0 else centre[:, :128]
    after = read(start + WIDE, 128) if start + WIDE < PLANE else centre[:, :128]
    return centre, before, after


def planes_kernel(magnet_ref, left_ref, right_ref, head_ref, tail_ref):
    for c in range(3):
        for i in range(SEEN):
            row = i
            if i == 0:
                source = left_ref.at[c]
            elif i == SEEN - 1:
                source = right_ref.at[c]
            else:
                source = magnet_ref.at[c, i - 1]
            head_ref[row, c : c + 1, :] = source[0:1, :]
            tail_ref[row, c : c + 1, :] = source[7:8, :]


def edge_planes(magnet, left, right):
    shape = jax.ShapeDtypeStruct((SEEN, 3, PLANE), F32)
    return pl.pallas_call(
        planes_kernel,
        out_shape=(shape, shape),
        name="edge_planes",
        compiler_params=pltpu.CompilerParams(vmem_limit_bytes=6 << 20),
    )(magnet, left, right)


def three_parts(values):
    top = values.astype(BF16).astype(F32)
    rest = values - top
    middle = rest.astype(BF16).astype(F32)
    return top, middle, rest - middle


def gather_sides(total_x, piece, k, half):
    kept = jnp.where(half == 0, piece, 0.0) + jnp.where(half == 32, pltpu.roll(piece, 33, 1), 0.0)
    return total_x + (pltpu.roll(kept, k, 1) if k else kept)


def write_block(rows_at, magnet_ref, out_ref, stage_ref):
    lane = lanes_of(128)
    half = lane & 63
    for p in range(OWN):
        side_x = jnp.zeros((8, 128), F32)
        side_y = jnp.zeros((8, 128), F32)
        spin_x = jnp.zeros((8, 128), F32)
        spin_y = jnp.zeros((8, 128), F32)
        for chunk in range(PLANE // WIDE):
            span = pl.ds(WIDE * chunk, WIDE)
            wide_lane = lanes_of(WIDE)
            x_at = wide_lane & 63
            y_at = (wide_lane + WIDE * chunk) >> 6
            east, west = neighbours_x(magnet_ref[0, p, :, span])
            north, south = neighbours_y(*sides(lambda s, w: magnet_ref[1, p, :, pl.ds(s, w)], chunk))
            spin = magnet_ref[2, p, :, span]
            nothing = jnp.zeros((1, WIDE), F32)
            upper, lower = neighbours_z(spin, nothing, nothing)
            diverge = 0.5 * (
                jnp.where(x_at < GRID - 1, east, 0.0)
                - jnp.where(x_at > 0, west, 0.0)
                + jnp.where(y_at < GRID - 1, north, 0.0)
                - jnp.where(y_at > 0, south, 0.0)
                + upper
                - lower
            )
            chosen = jnp.where(rows_at == 0, diverge[0:1], diverge[7:8])
            for j in range(WIDE // 256):
                at = 32 + 4 * (chunk * (WIDE // 256) + j) + p
                stage_ref[at : at + 1, :] = chosen[:, 256 * j : 256 * j + 256]
            for j in range(WIDE // 128):
                k = chunk * (WIDE // 128) + j
                side_x = gather_sides(side_x, diverge[:, 128 * j : 128 * j + 128], k, half)
                spin_x = gather_sides(spin_x, spin[:, 128 * j : 128 * j + 128], k, half)
            if chunk == 0:
                side_y = diverge[:, :128]
                spin_y = spin[:, :128]
            if chunk == PLANE // WIDE - 1:
                side_y = jnp.where(lane < 64, side_y, diverge[:, WIDE - 128 :])
                spin_y = jnp.where(lane < 64, spin_y, spin[:, WIDE - 128 :])
        cycle = jnp.concatenate([side_y, side_x], axis=1)
        for z in range(PLANES):
            stage_ref[4 * z + p : 4 * z + p + 1, :] = cycle[z : z + 1]
        parts = three_parts(cycle) + three_parts(jnp.concatenate([spin_y, spin_x], axis=1))
        for n in range(6):
            for end in range(2):
                at = 96 + 24 * end + 4 * n + p
                stage_ref[at : at + 1, :] = parts[n][7 * end : 7 * end + 1]
    whole = stage_ref[...].astype(BF16)
    for r in range(ROWS):
        out_ref[r] = whole


def surface_kernel(at_ref, magnet_ref, out_ref, stage_ref):
    write_block(at_ref[0], magnet_ref, out_ref, stage_ref)


def surface_block(at, magnet):
    return pl.pallas_call(
        surface_kernel,
        in_specs=[pl.BlockSpec(memory_space=pltpu.SMEM), pl.BlockSpec(memory_space=pltpu.VMEM)],
        out_shape=jax.ShapeDtypeStruct((ROWS, BLOCK, 256), BF16),
        scratch_shapes=[pltpu.VMEM((BLOCK, 256), F32)],
        name="surface_block",
        compiler_params=pltpu.CompilerParams(vmem_limit_bytes=8 << 20),
    )(at, magnet)


def lane_choice(low):
    lane = lax.broadcasted_iota(jnp.int32, (256, low.shape[1]), 0)
    return jnp.where(lane == low, 1.0, 0.0).astype(BF16)


def trace_kernel(table_ref, low_ref, high_ref, out_ref, whole_ref):
    ends = [table_ref[slab, 96:BLOCK, :].astype(F32) for slab in range(ROWS)]

    def joined(slab, end, first):
        at = 24 * end + 4 * first
        part = ends[slab]
        return part[at : at + 4] + (part[at + 4 : at + 8] + part[at + 8 : at + 12])

    for slab in range(ROWS):
        base = 32 * slab
        whole_ref[base : base + 32, :] = table_ref[slab, 0:32, :].astype(F32)
        if slab > 0:
            whole_ref[base : base + 4, :] = joined(slab, 0, 0) - 0.5 * joined(slab - 1, 1, 3)
        if slab < ROWS - 1:
            whole_ref[base + 28 : base + 32, :] = joined(slab, 1, 0) + 0.5 * joined(slab + 1, 0, 3)
    whole_ref[256:320, :] = table_ref[0, 32:96, :].astype(F32)
    whole_ref[320:384, :] = table_ref[ROWS - 1, 32:96, :].astype(F32)
    table = whole_ref[...].astype(BF16)
    width = 2 * PIECE
    for tile in range(COLS // 2):
        low = low_ref[:, width * tile : width * tile + width]
        high = high_ref[:, width * tile : width * tile + width]
        picked = jnp.dot(table, lane_choice(low), preferred_element_type=F32)
        offset = high - (lax.broadcasted_iota(jnp.int32, (8, width), 0) >> 2)
        total = jnp.zeros((8, width), F32)
        for pair in range(48):
            total = total + jnp.where(offset == 2 * pair, picked[8 * pair : 8 * pair + 8], 0.0)
        found = (total[0:4] + total[4:8]).astype(BF16)
        for r in range(ROWS):
            out_ref[COLS * r + 2 * tile] = found[:, :PIECE]
            out_ref[COLS * r + 2 * tile + 1] = found[:, PIECE:]


def take_trace(table, low, high):
    return pl.pallas_call(
        trace_kernel,
        out_shape=jax.ShapeDtypeStruct((ROWS * COLS, OWN, PIECE), BF16),
        scratch_shapes=[pltpu.VMEM((384, 256), F32)],
        name="take_trace",
        compiler_params=pltpu.CompilerParams(vmem_limit_bytes=12 << 20),
    )(table, low, high)


def partial_kernel(owned_ref, matrix_ref, out_ref, traced_ref, rows_ref, stage_ref):
    @pl.when(pl.program_id(0) == 0)
    def _():
        for r in range(COL_BLOCK // PIECE):
            for c in range(COLS):
                traced_ref[OWN * c : OWN * c + OWN, PIECE * r : PIECE * r + PIECE] = owned_ref[
                    COLS * r + c
                ].astype(F32)
        rows_ref[0:8, :] = jnp.zeros((8, 256), F32)
        rows_ref[72:80, :] = jnp.zeros((8, 256), F32)

    traced = traced_ref[...].astype(BF16)
    for part in range(TOGETHER):
        rows_ref[8:72, :] = lax.dot_general(
            traced,
            matrix_ref[256 * part : 256 * part + 256, :],
            (((1,), (1,)), ((), ())),
            preferred_element_type=F32,
        )
        for c in range(COLS):
            first = 7 + OWN * c
            for side in range(2):
                at = (2 * part + side) * SEEN
                stage_ref[c, at : at + SEEN, :] = rows_ref[
                    first : first + SEEN, 128 * side : 128 * side + 128
                ]
    out_ref[...] = stage_ref[...].astype(out_ref.dtype)


def partial_potential(owned, matrix):
    rows = 2 * TOGETHER * SEEN
    return pl.pallas_call(
        partial_kernel,
        grid=(CHUNKS // TOGETHER,),
        in_specs=[
            pl.BlockSpec((ROWS * COLS, OWN, PIECE), lambda i: (0, 0, 0)),
            pl.BlockSpec((256 * TOGETHER, COL_BLOCK), lambda i: (i, 0)),
        ],
        out_specs=pl.BlockSpec((COLS, rows, 128), lambda i: (0, i, 0)),
        out_shape=jax.ShapeDtypeStruct((COLS, 2 * CHUNKS * SEEN, 128), PART),
        scratch_shapes=[
            pltpu.VMEM((64, COL_BLOCK), F32),
            pltpu.VMEM((80, 256), F32),
            pltpu.VMEM((COLS, rows, 128), F32),
        ],
        name="partial_potential",
        compiler_params=pltpu.CompilerParams(vmem_limit_bytes=55 << 20),
    )(owned, matrix)


def combine_kernel(parts_ref, out_ref, sum_ref):
    total = parts_ref[0].astype(F32)
    for c in range(1, COLS):
        total = total + parts_ref[c].astype(F32)
    sum_ref[0 : 2 * CHUNKS * SEEN, :] = total
    sum_ref[2 * CHUNKS * SEEN :, :] = jnp.zeros((8, 128), F32)
    halves = [
        jnp.concatenate(
            [sum_ref[SEEN * (2 * h + side) : SEEN * (2 * h + side) + 8, :] for h in range(CHUNKS)], axis=0
        )
        for side in range(2)
    ]
    rows = jnp.concatenate(halves, axis=1).astype(out_ref.dtype)
    for r in range(ROWS):
        out_ref[r] = rows


def combine(parts):
    return pl.pallas_call(
        combine_kernel,
        out_shape=jax.ShapeDtypeStruct((ROWS, 8 * CHUNKS, 256), POT),
        scratch_shapes=[pltpu.VMEM((2 * CHUNKS * SEEN + 8, 128), F32)],
        name="combine",
        compiler_params=pltpu.CompilerParams(vmem_limit_bytes=6 << 20),
    )(parts)


def exchange_field(rows_at, source_ref, below_ref, above_ref, out_ref):
    for chunk in range(PLANE // WIDE):
        span = pl.ds(WIDE * chunk, WIDE)
        wide_lane = lanes_of(WIDE)
        x_at = wide_lane & 63
        y_at = (wide_lane + WIDE * chunk) >> 6
        centre, before, after = sides(lambda s, w: source_ref[:, pl.ds(s, w)], chunk)
        east, west = neighbours_x(centre)
        north, south = neighbours_y(centre, before, after)
        upper, lower = neighbours_z(
            centre,
            jnp.where(rows_at == 0, centre[0:1], below_ref[:, span]),
            jnp.where(rows_at == ROWS - 1, centre[7:8], above_ref[:, span]),
        )
        total = (
            jnp.where(x_at < GRID - 1, east, centre)
            + jnp.where(x_at > 0, west, centre)
            + jnp.where(y_at < GRID - 1, north, centre)
            + jnp.where(y_at > 0, south, centre)
            + upper
            + lower
        )
        out_ref[:, span] = exchange_coef * (total - 6.0 * centre)


def find_returned(table_ref, low_ref, high_ref, found_ref, cycle_ref):
    table = table_ref[...].reshape(ROWS * 8 * CHUNKS, 256)
    for tile in range(12):
        low = low_ref[:, 512 * tile : 512 * tile + 512]
        high = high_ref[:, 512 * tile : 512 * tile + 512]
        choice = lane_choice(low)
        if POT == BF16:
            picked = jnp.dot(table, choice, preferred_element_type=F32)
        else:
            top = table.astype(BF16)
            rest = (table - top.astype(F32)).astype(BF16)
            picked = jnp.dot(top, choice, preferred_element_type=F32) + jnp.dot(
                rest, choice, preferred_element_type=F32
            )
        high = jnp.broadcast_to(high, (8, 512))
        total = jnp.zeros((8, 512), F32)
        for h in range(ROWS * CHUNKS):
            total = total + jnp.where(high == h, picked[8 * h : 8 * h + 8], 0.0)
        total = demag_coef * total
        if tile < 4:
            for z in range(2):
                for p in range(SEEN):
                    cycle_ref[p, 2 * tile + z : 2 * tile + z + 1, :] = total[
                        p : p + 1, 256 * z : 256 * z + 256
                    ]
        else:
            for p in range(SEEN):
                found_ref[p, :, 512 * (tile - 4) : 512 * (tile - 3)] = total[p : p + 1]


def torque_kernel(
    at_ref, table_ref, low_ref, high_ref, magnet_ref, below_ref, above_ref, left_ref, right_ref,
    out_ref, sums_ref, field_ref, found_ref, cycle_ref, near_ref, far_ref,
):
    rows_at = at_ref[0]
    find_returned(table_ref, low_ref, high_ref, found_ref, cycle_ref)
    lane = lanes_of(128)
    half = lane & 63
    plane_at = lax.broadcasted_iota(jnp.int32, (8, 128), 0)
    sign = jnp.where(
        (plane_at == 0) & (rows_at == 0),
        1.0,
        jnp.where((plane_at == 7) & (rows_at == ROWS - 1), -1.0, 0.0),
    )

    def image(i, sources):
        for c in range(3):
            exchange_field(
                rows_at, sources[c], below_ref.at[i, c : c + 1], above_ref.at[i, c : c + 1], field_ref.at[c]
            )
        side_y = cycle_ref[i, :, 0:128]
        side_x = cycle_ref[i, :, 128:256]
        near = jnp.zeros((8, 128), F32)
        far = jnp.zeros((8, 128), F32)
        last = jnp.maximum(i - 1, 0)
        second = jnp.maximum(i - 2, 0)
        for k in range(PLANE // 128):
            span = pl.ds(128 * k, 128)
            m = [sources[c][:, span] for c in range(3)]
            f = [field_ref[c, :, span] for c in range(3)]
            rolled = pltpu.roll(side_x, 128 - k, 1) if k else side_x
            f[0] = (
                f[0]
                + jnp.where(half == 0, rolled, 0.0)
                - jnp.where(half == 63, pltpu.roll(side_x, 95 - k, 1), 0.0)
            )
            if k == 0:
                f[1] = f[1] + jnp.where(lane < 64, side_y, 0.0)
            if k == PLANE // 128 - 1:
                f[1] = f[1] - jnp.where(lane >= 64, side_y, 0.0)
            f[2] = f[2] + sign * found_ref[i, :, span]
            along = m[0] * f[0] + m[1] * f[1] + m[2] * f[2]
            length = m[0] * m[0] + m[1] * m[1] + m[2] * m[2]
            v = [m[c] - time_step * (m[c] * along - f[c] * length) for c in range(3)]
            scale = lax.rsqrt(v[0] * v[0] + v[1] * v[1] + v[2] * v[2])
            for c in range(3):
                t = v[c] * scale
                out_ref[i, c, :, span] = t
                step = t - out_ref[last, c, :, span]
                near = near + step * step
                step = t - out_ref[second, c, :, span]
                far = far + step * step
        near_ref[i] = near
        far_ref[i] = far

    def own(i, carry):
        image(i, [magnet_ref.at[c, i - 1] for c in range(3)])
        return carry

    image(0, [left_ref.at[c] for c in range(3)])
    lax.fori_loop(1, SEEN - 1, own, 0)
    image(SEEN - 1, [right_ref.at[c] for c in range(3)])
    blank = jnp.zeros((2, 128), F32)
    sums = jnp.concatenate(
        [jnp.sum(near_ref[n], axis=0, keepdims=True) for n in range(SEEN)]
        + [blank]
        + [jnp.sum(far_ref[n], axis=0, keepdims=True) for n in range(SEEN)]
        + [blank],
        axis=0,
    )
    for r in range(ROWS):
        sums_ref[r] = sums


def torque(at, table, low, high, magnet, below, above, left, right):
    vmem = pl.BlockSpec(memory_space=pltpu.VMEM)
    return pl.pallas_call(
        torque_kernel,
        in_specs=[pl.BlockSpec(memory_space=pltpu.SMEM)] + [vmem] * 8,
        out_specs=(vmem, vmem),
        out_shape=(
            jax.ShapeDtypeStruct((SEEN, 3, PLANES, PLANE), F32),
            jax.ShapeDtypeStruct((ROWS, 16, 128), F32),
        ),
        scratch_shapes=[
            pltpu.VMEM((3, PLANES, PLANE), F32),
            pltpu.VMEM((SEEN, 1, PLANE), F32),
            pltpu.VMEM((SEEN, 8, 256), F32),
            pltpu.VMEM((SEEN, 8, 128), F32),
            pltpu.VMEM((SEEN, 8, 128), F32),
        ],
        name="torque",
        compiler_params=pltpu.CompilerParams(vmem_limit_bytes=20 << 20),
    )(at, table, low, high, magnet, below, above, left, right)


def tension_kernel(at_ref, sums_ref, torqued_ref, out_ref, *more):
    cols_at = at_ref[1]
    total = sums_ref[0]
    for r in range(1, ROWS):
        total = total + sums_ref[r]
    total = jnp.sum(total, axis=1, keepdims=True)
    root = jnp.sqrt(total * (1.0 / entries) + 1e-06)
    for p in range(OWN):
        j = p + 1
        coefficient = spring_coef * (root[j + 1 : j + 2] - root[j : j + 1])
        scale = jnp.broadcast_to(coefficient / root[9 + j : 10 + j], (8, 128))
        if p == 0:
            free = cols_at > 0
        elif p == OWN - 1:
            free = cols_at < COLS - 1
        else:
            free = None

        def lanes(k, carry):
            span = pl.ds(pl.multiple_of(128 * k, 128), 128)
            t = [torqued_ref[j, c, :, span] for c in range(3)]
            force = [
                (torqued_ref[j + 1, c, :, span] - torqued_ref[j - 1, c, :, span]) * scale
                for c in range(3)
            ]
            along = force[0] * t[0] + force[1] * t[1] + force[2] * t[2]
            w = [t[c] + force[c] - along * t[c] for c in range(3)]
            size = lax.rsqrt(w[0] * w[0] + w[1] * w[1] + w[2] * w[2])
            for c in range(3):
                new = w[c] * size
                if free is not None:
                    new = jnp.where(free, new, t[c])
                out_ref[c, p, :, span] = new
            return carry

        lax.fori_loop(0, PLANE // 128, lanes, 0, unroll=4)
    if more:
        write_block(at_ref[0], out_ref, *more)


def tension(at, sums, torqued, with_block):
    vmem = pl.BlockSpec(memory_space=pltpu.VMEM)
    block = jax.ShapeDtypeStruct((ROWS, BLOCK, 256), BF16)
    return pl.pallas_call(
        tension_kernel,
        in_specs=[pl.BlockSpec(memory_space=pltpu.SMEM), vmem, vmem],
        out_shape=(jax.ShapeDtypeStruct((3, OWN, PLANES, PLANE), F32),) + ((block,) if with_block else ()),
        scratch_shapes=[pltpu.VMEM((BLOCK, 256), F32)] if with_block else [],
        name="tension",
        compiler_params=pltpu.CompilerParams(vmem_limit_bytes=10 << 20),
    )(at, sums, torqued)


def swap(values, axis):
    return lax.all_to_all(values, axis, split_axis=0, concat_axis=0, tiled=True)


def up(values, axis):
    return lax.ppermute(values, axis, [(i, i + 1) for i in range(lax.axis_size(axis) - 1)])


def down(values, axis):
    return lax.ppermute(values, axis, [(i + 1, i) for i in range(lax.axis_size(axis) - 1)])


def trace_positions(trace_slot, rows_at):
    piece = jnp.minimum(rows_at, COL_BLOCK // PIECE - 1)
    mine = lax.dynamic_slice(
        trace_slot.reshape(COLS, COL_BLOCK), (0, piece * PIECE), (COLS, PIECE)
    )
    high = mine >> 8
    low = mine & 255
    k = (low & 63) >> 1
    odd = low & 1
    far = (low >> 6) & 1
    lane = k + jnp.where(far == 0, odd * 64, 96 - odd * 64)
    low = jnp.where((high < GRID) & (low >= 128), 128 + lane, low)
    return low.reshape(1, COLS * PIECE), high.reshape(1, COLS * PIECE)


def return_positions(return_row, rows_at):
    cycles = lax.dynamic_slice_in_dim(return_row, rows_at * PLANES * 256, PLANES * 256)
    plane = jnp.where(rows_at == 0, return_row[16384:20480], return_row[20480:])
    both = jnp.stack([cycles & 255, cycles >> 8]).reshape(2 * PLANES, 256)
    place = jnp.arange(128, dtype=jnp.int32)
    k = place & 31
    source = jnp.where(
        place < 32, 2 * k, jnp.where(place < 64, 65 + 2 * k, jnp.where(place < 96, 2 * k + 1, 64 + 2 * k))
    )
    order = (source[None, :] == place[:, None]).astype(BF16)
    turned = jnp.dot(both[:, 128:].astype(BF16), order, preferred_element_type=F32).astype(jnp.int32)
    both = jnp.concatenate([both[:, :128], turned], axis=1).reshape(2, PLANES * 256)
    low = jnp.concatenate([both[0], plane & 255])
    high = jnp.concatenate([both[1], plane >> 8])
    return low.reshape(1, -1), high.reshape(1, -1)


def body(m_start, boundary_matrix, trace_slot, return_row):
    rows_at = lax.axis_index("rows")
    cols_at = lax.axis_index("cols")
    at = jnp.stack([rows_at, cols_at]).astype(jnp.int32)
    trace_at = trace_positions(trace_slot, rows_at)
    return_at = return_positions(return_row, rows_at)
    magnet = m_start
    block = surface_block(at, magnet)
    for repeat_at in range(STEPS):
        table = swap(block, "rows")
        from_left = up(magnet[:, OWN - 1], "cols")
        from_right = down(magnet[:, 0], "cols")
        traced = take_trace(table, *trace_at)
        owned = swap(traced, ("rows", "cols"))
        owned, from_left, from_right = lax.optimization_barrier((owned, from_left, from_right))
        head, tail = edge_planes(magnet, from_left, from_right)
        parts = swap(partial_potential(owned, boundary_matrix), "cols")
        below = up(tail, "rows")
        above = down(head, "rows")
        mine, below, above = lax.optimization_barrier((combine(parts), below, above))
        potential = swap(mine, "rows")
        torqued, sums = torque(at, potential, *return_at, magnet, below, above, from_left, from_right)
        sums = swap(sums, "rows")
        made = tension(at, sums, torqued, repeat_at + 1 < STEPS)
        magnet = made[0]
        block = made[-1]
    return magnet


def solution(mesh):
    return jax.shard_map(
        body,
        mesh=mesh,
        in_specs=(P(None, "cols", "rows", None), P("rows", "cols"), P(), P()),
        out_specs=P(None, "cols", "rows", None),
        check_vma=False,
    )
```

```python
import jax
import jax.numpy as jnp
from jax import lax
from jax.experimental import pallas as pl
from jax.experimental.pallas import tpu as pltpu
from jax.sharding import PartitionSpec as P

GRID = 64
STEPS = 2
ROWS = 8
COLS = 16
NB = 24576
PLANES = 8
PLANE = GRID * GRID
COL_BLOCK = NB // COLS
CHUNKS = NB // ROWS // 256
OWN = 4
BLOCK = 144
SEEN = 6
PIECE = 256
WIDE = 1024
F32 = jnp.float32
BF16 = jnp.bfloat16
POT = BF16

exchange_coef = 0.25
demag_coef = 2.0
time_step = 0.2
spring_coef = 2.0
entries = 3.0 * GRID * GRID * GRID


def lanes_of(width):
    return lax.broadcasted_iota(jnp.int32, (8, width), 1)


def neighbours_y(values, before, after):
    width = values.shape[1]
    whole = jnp.concatenate([before, values, after], axis=1)
    pieces = [pltpu.roll(whole[:, 128 * k : 128 * k + 128], 64, 1) for k in range(width // 128 + 2)]
    low = lanes_of(128) < 64
    north = [jnp.where(low, pieces[k + 1], pieces[k + 2]) for k in range(width // 128)]
    south = [jnp.where(low, pieces[k], pieces[k + 1]) for k in range(width // 128)]
    return jnp.concatenate(north, axis=1), jnp.concatenate(south, axis=1)


def neighbours_x(values):
    pieces = [values[:, 128 * k : 128 * k + 128] for k in range(values.shape[1] // 128)]
    east = jnp.concatenate([pltpu.roll(piece, 127, 1) for piece in pieces], axis=1)
    west = jnp.concatenate([pltpu.roll(piece, 1, 1) for piece in pieces], axis=1)
    return east, west


def neighbours_z(values, below, above):
    width = values.shape[1]
    plane = lax.broadcasted_iota(jnp.int32, (8, width), 0)
    upper = jnp.where(plane == 7, jnp.broadcast_to(above, (8, width)), pltpu.roll(values, 7, 0))
    lower = jnp.where(plane == 0, jnp.broadcast_to(below, (8, width)), pltpu.roll(values, 1, 0))
    return upper, lower


def sides(read, chunk):
    start = WIDE * chunk
    centre = read(start, WIDE)
    before = read(start - 128, 128) if chunk > 0 else centre[:, :128]
    after = read(start + WIDE, 128) if start + WIDE < PLANE else centre[:, :128]
    return centre, before, after


def planes_kernel(magnet_ref, left_ref, right_ref, head_ref, tail_ref):
    for c in range(3):
        for i in range(SEEN):
            row = i
            if i == 0:
                source = left_ref.at[c]
            elif i == SEEN - 1:
                source = right_ref.at[c]
            else:
                source = magnet_ref.at[c, i - 1]
            head_ref[row, c : c + 1, :] = source[0:1, :]
            tail_ref[row, c : c + 1, :] = source[7:8, :]


def edge_planes(magnet, left, right):
    shape = jax.ShapeDtypeStruct((SEEN, 3, PLANE), F32)
    return pl.pallas_call(
        planes_kernel,
        out_shape=(shape, shape),
        name="edge_planes",
        compiler_params=pltpu.CompilerParams(vmem_limit_bytes=6 << 20),
    )(magnet, left, right)


def three_parts(values):
    top = values.astype(BF16).astype(F32)
    rest = values - top
    middle = rest.astype(BF16).astype(F32)
    return top, middle, rest - middle


def gather_sides(total_x, piece, k, half):
    kept = jnp.where(half == 0, piece, 0.0) + jnp.where(half == 32, pltpu.roll(piece, 33, 1), 0.0)
    return total_x + (pltpu.roll(kept, k, 1) if k else kept)


def write_block(rows_at, magnet_ref, out_ref, stage_ref):
    lane = lanes_of(128)
    half = lane & 63
    for p in range(OWN):
        side_x = jnp.zeros((8, 128), F32)
        side_y = jnp.zeros((8, 128), F32)
        spin_x = jnp.zeros((8, 128), F32)
        spin_y = jnp.zeros((8, 128), F32)
        for chunk in range(PLANE // WIDE):
            span = pl.ds(WIDE * chunk, WIDE)
            wide_lane = lanes_of(WIDE)
            x_at = wide_lane & 63
            y_at = (wide_lane + WIDE * chunk) >> 6
            east, west = neighbours_x(magnet_ref[0, p, :, span])
            north, south = neighbours_y(*sides(lambda s, w: magnet_ref[1, p, :, pl.ds(s, w)], chunk))
            spin = magnet_ref[2, p, :, span]
            nothing = jnp.zeros((1, WIDE), F32)
            upper, lower = neighbours_z(spin, nothing, nothing)
            diverge = 0.5 * (
                jnp.where(x_at < GRID - 1, east, 0.0)
                - jnp.where(x_at > 0, west, 0.0)
                + jnp.where(y_at < GRID - 1, north, 0.0)
                - jnp.where(y_at > 0, south, 0.0)
                + upper
                - lower
            )
            chosen = jnp.where(rows_at == 0, diverge[0:1], diverge[7:8])
            for j in range(WIDE // 256):
                at = 32 + 4 * (chunk * (WIDE // 256) + j) + p
                stage_ref[at : at + 1, :] = chosen[:, 256 * j : 256 * j + 256]
            for j in range(WIDE // 128):
                k = chunk * (WIDE // 128) + j
                side_x = gather_sides(side_x, diverge[:, 128 * j : 128 * j + 128], k, half)
                spin_x = gather_sides(spin_x, spin[:, 128 * j : 128 * j + 128], k, half)
            if chunk == 0:
                side_y = diverge[:, :128]
                spin_y = spin[:, :128]
            if chunk == PLANE // WIDE - 1:
                side_y = jnp.where(lane < 64, side_y, diverge[:, WIDE - 128 :])
                spin_y = jnp.where(lane < 64, spin_y, spin[:, WIDE - 128 :])
        cycle = jnp.concatenate([side_y, side_x], axis=1)
        for z in range(PLANES):
            stage_ref[4 * z + p : 4 * z + p + 1, :] = cycle[z : z + 1]
        parts = three_parts(cycle) + three_parts(jnp.concatenate([spin_y, spin_x], axis=1))
        for n in range(6):
            for end in range(2):
                at = 96 + 24 * end + 4 * n + p
                stage_ref[at : at + 1, :] = parts[n][7 * end : 7 * end + 1]
    whole = stage_ref[...].astype(BF16)
    for r in range(ROWS):
        out_ref[r] = whole


def surface_kernel(at_ref, magnet_ref, out_ref, stage_ref):
    write_block(at_ref[0], magnet_ref, out_ref, stage_ref)


def surface_block(at, magnet):
    return pl.pallas_call(
        surface_kernel,
        in_specs=[pl.BlockSpec(memory_space=pltpu.SMEM), pl.BlockSpec(memory_space=pltpu.VMEM)],
        out_shape=jax.ShapeDtypeStruct((ROWS, BLOCK, 256), BF16),
        scratch_shapes=[pltpu.VMEM((BLOCK, 256), F32)],
        name="surface_block",
        compiler_params=pltpu.CompilerParams(vmem_limit_bytes=8 << 20),
    )(at, magnet)


def lane_choice(low):
    lane = lax.broadcasted_iota(jnp.int32, (256, low.shape[1]), 0)
    return jnp.where(lane == low, 1.0, 0.0).astype(BF16)


def trace_kernel(table_ref, low_ref, high_ref, out_ref, whole_ref):
    ends = [table_ref[slab, 96:BLOCK, :].astype(F32) for slab in range(ROWS)]

    def joined(slab, end, first):
        at = 24 * end + 4 * first
        part = ends[slab]
        return part[at : at + 4] + (part[at + 4 : at + 8] + part[at + 8 : at + 12])

    for slab in range(ROWS):
        base = 32 * slab
        whole_ref[base : base + 32, :] = table_ref[slab, 0:32, :].astype(F32)
        if slab > 0:
            whole_ref[base : base + 4, :] = joined(slab, 0, 0) - 0.5 * joined(slab - 1, 1, 3)
        if slab < ROWS - 1:
            whole_ref[base + 28 : base + 32, :] = joined(slab, 1, 0) + 0.5 * joined(slab + 1, 0, 3)
    whole_ref[256:320, :] = table_ref[0, 32:96, :].astype(F32)
    whole_ref[320:384, :] = table_ref[ROWS - 1, 32:96, :].astype(F32)
    table = whole_ref[...].astype(BF16)
    width = 2 * PIECE
    for tile in range(COLS // 2):
        low = low_ref[:, width * tile : width * tile + width]
        high = high_ref[:, width * tile : width * tile + width]
        picked = jnp.dot(table, lane_choice(low), preferred_element_type=F32)
        offset = high - (lax.broadcasted_iota(jnp.int32, (8, width), 0) >> 2)
        total = jnp.zeros((8, width), F32)
        for pair in range(48):
            total = total + jnp.where(offset == 2 * pair, picked[8 * pair : 8 * pair + 8], 0.0)
        found = (total[0:4] + total[4:8]).astype(BF16)
        for r in range(ROWS):
            out_ref[COLS * r + 2 * tile] = found[:, :PIECE]
            out_ref[COLS * r + 2 * tile + 1] = found[:, PIECE:]


def take_trace(table, low, high):
    return pl.pallas_call(
        trace_kernel,
        out_shape=jax.ShapeDtypeStruct((ROWS * COLS, OWN, PIECE), BF16),
        scratch_shapes=[pltpu.VMEM((384, 256), F32)],
        name="take_trace",
        compiler_params=pltpu.CompilerParams(vmem_limit_bytes=12 << 20),
    )(table, low, high)


def partial_kernel(owned_ref, matrix_ref, out_ref, traced_ref, rows_ref):
    for r in range(COL_BLOCK // PIECE):
        for c in range(COLS):
            traced_ref[OWN * c : OWN * c + OWN, PIECE * r : PIECE * r + PIECE] = owned_ref[
                COLS * r + c
            ].astype(F32)
    traced = traced_ref[...].astype(BF16)
    for side in range(2):
        rows_ref[side, 0:8, :] = jnp.zeros((8, 256), F32)
        rows_ref[side, 72:80, :] = jnp.zeros((8, 256), F32)
    for h in range(CHUNKS):
        rows_ref[h % 2, 8:72, :] = lax.dot_general(
            traced,
            matrix_ref[256 * h : 256 * h + 256, :],
            (((1,), (1,)), ((), ())),
            preferred_element_type=F32,
        )
        for c in range(COLS):
            first = 7 + OWN * c
            for side in range(2):
                at = (2 * h + side) * SEEN
                out_ref[c, at : at + SEEN, :] = rows_ref[
                    h % 2, first : first + SEEN, 128 * side : 128 * side + 128
                ]


def partial_potential(owned, matrix):
    vmem = pl.BlockSpec(memory_space=pltpu.VMEM)
    return pl.pallas_call(
        partial_kernel,
        in_specs=[vmem, vmem],
        out_specs=vmem,
        out_shape=jax.ShapeDtypeStruct((COLS, 2 * CHUNKS * SEEN, 128), F32),
        scratch_shapes=[pltpu.VMEM((64, COL_BLOCK), F32), pltpu.VMEM((2, 80, 256), F32)],
        name="partial_potential",
        compiler_params=pltpu.CompilerParams(vmem_limit_bytes=14 << 20),
    )(owned, matrix)


def combine_kernel(parts_ref, out_ref, sum_ref):
    total = parts_ref[0].astype(F32)
    for c in range(1, COLS):
        total = total + parts_ref[c].astype(F32)
    sum_ref[0 : 2 * CHUNKS * SEEN, :] = total
    sum_ref[2 * CHUNKS * SEEN :, :] = jnp.zeros((8, 128), F32)
    halves = [
        jnp.concatenate(
            [sum_ref[SEEN * (2 * h + side) : SEEN * (2 * h + side) + 8, :] for h in range(CHUNKS)], axis=0
        )
        for side in range(2)
    ]
    rows = jnp.concatenate(halves, axis=1).astype(out_ref.dtype)
    for r in range(ROWS):
        out_ref[r] = rows


def combine(parts):
    return pl.pallas_call(
        combine_kernel,
        out_shape=jax.ShapeDtypeStruct((ROWS, 8 * CHUNKS, 256), POT),
        scratch_shapes=[pltpu.VMEM((2 * CHUNKS * SEEN + 8, 128), F32)],
        name="combine",
        compiler_params=pltpu.CompilerParams(vmem_limit_bytes=6 << 20),
    )(parts)


def exchange_field(rows_at, source_ref, below_ref, above_ref, out_ref):
    for chunk in range(PLANE // WIDE):
        span = pl.ds(WIDE * chunk, WIDE)
        wide_lane = lanes_of(WIDE)
        x_at = wide_lane & 63
        y_at = (wide_lane + WIDE * chunk) >> 6
        centre, before, after = sides(lambda s, w: source_ref[:, pl.ds(s, w)], chunk)
        east, west = neighbours_x(centre)
        north, south = neighbours_y(centre, before, after)
        upper, lower = neighbours_z(
            centre,
            jnp.where(rows_at == 0, centre[0:1], below_ref[:, span]),
            jnp.where(rows_at == ROWS - 1, centre[7:8], above_ref[:, span]),
        )
        total = (
            jnp.where(x_at < GRID - 1, east, centre)
            + jnp.where(x_at > 0, west, centre)
            + jnp.where(y_at < GRID - 1, north, centre)
            + jnp.where(y_at > 0, south, centre)
            + upper
            + lower
        )
        out_ref[:, span] = exchange_coef * (total - 6.0 * centre)


def find_returned(table_ref, low_ref, high_ref, found_ref, cycle_ref):
    table = table_ref[...].reshape(ROWS * 8 * CHUNKS, 256)
    for tile in range(12):
        low = low_ref[:, 512 * tile : 512 * tile + 512]
        high = high_ref[:, 512 * tile : 512 * tile + 512]
        choice = lane_choice(low)
        if POT == BF16:
            picked = jnp.dot(table, choice, preferred_element_type=F32)
        else:
            top = table.astype(BF16)
            rest = (table - top.astype(F32)).astype(BF16)
            picked = jnp.dot(top, choice, preferred_element_type=F32) + jnp.dot(
                rest, choice, preferred_element_type=F32
            )
        high = jnp.broadcast_to(high, (8, 512))
        total = jnp.zeros((8, 512), F32)
        for h in range(ROWS * CHUNKS):
            total = total + jnp.where(high == h, picked[8 * h : 8 * h + 8], 0.0)
        total = demag_coef * total
        if tile < 4:
            for z in range(2):
                for p in range(SEEN):
                    cycle_ref[p, 2 * tile + z : 2 * tile + z + 1, :] = total[
                        p : p + 1, 256 * z : 256 * z + 256
                    ]
        else:
            for p in range(SEEN):
                found_ref[p, :, 512 * (tile - 4) : 512 * (tile - 3)] = total[p : p + 1]


def torque_kernel(
    at_ref, table_ref, low_ref, high_ref, magnet_ref, below_ref, above_ref, left_ref, right_ref,
    out_ref, sums_ref, field_ref, found_ref, cycle_ref, near_ref, far_ref,
):
    rows_at = at_ref[0]
    find_returned(table_ref, low_ref, high_ref, found_ref, cycle_ref)
    lane = lanes_of(128)
    half = lane & 63
    plane_at = lax.broadcasted_iota(jnp.int32, (8, 128), 0)
    sign = jnp.where(
        (plane_at == 0) & (rows_at == 0),
        1.0,
        jnp.where((plane_at == 7) & (rows_at == ROWS - 1), -1.0, 0.0),
    )

    def image(i, sources):
        for c in range(3):
            exchange_field(
                rows_at, sources[c], below_ref.at[i, c : c + 1], above_ref.at[i, c : c + 1], field_ref.at[c]
            )
        side_y = cycle_ref[i, :, 0:128]
        side_x = cycle_ref[i, :, 128:256]
        near = jnp.zeros((8, 128), F32)
        far = jnp.zeros((8, 128), F32)
        last = jnp.maximum(i - 1, 0)
        second = jnp.maximum(i - 2, 0)
        for k in range(PLANE // 128):
            span = pl.ds(128 * k, 128)
            m = [sources[c][:, span] for c in range(3)]
            f = [field_ref[c, :, span] for c in range(3)]
            rolled = pltpu.roll(side_x, 128 - k, 1) if k else side_x
            f[0] = (
                f[0]
                + jnp.where(half == 0, rolled, 0.0)
                - jnp.where(half == 63, pltpu.roll(side_x, 95 - k, 1), 0.0)
            )
            if k == 0:
                f[1] = f[1] + jnp.where(lane < 64, side_y, 0.0)
            if k == PLANE // 128 - 1:
                f[1] = f[1] - jnp.where(lane >= 64, side_y, 0.0)
            f[2] = f[2] + sign * found_ref[i, :, span]
            along = m[0] * f[0] + m[1] * f[1] + m[2] * f[2]
            length = m[0] * m[0] + m[1] * m[1] + m[2] * m[2]
            v = [m[c] - time_step * (m[c] * along - f[c] * length) for c in range(3)]
            scale = lax.rsqrt(v[0] * v[0] + v[1] * v[1] + v[2] * v[2])
            for c in range(3):
                t = v[c] * scale
                out_ref[i, c, :, span] = t
                step = t - out_ref[last, c, :, span]
                near = near + step * step
                step = t - out_ref[second, c, :, span]
                far = far + step * step
        near_ref[i] = near
        far_ref[i] = far

    def own(i, carry):
        image(i, [magnet_ref.at[c, i - 1] for c in range(3)])
        return carry

    image(0, [left_ref.at[c] for c in range(3)])
    lax.fori_loop(1, SEEN - 1, own, 0)
    image(SEEN - 1, [right_ref.at[c] for c in range(3)])
    blank = jnp.zeros((2, 128), F32)
    sums = jnp.concatenate(
        [jnp.sum(near_ref[n], axis=0, keepdims=True) for n in range(SEEN)]
        + [blank]
        + [jnp.sum(far_ref[n], axis=0, keepdims=True) for n in range(SEEN)]
        + [blank],
        axis=0,
    )
    for r in range(ROWS):
        sums_ref[r] = sums


def torque(at, table, low, high, magnet, below, above, left, right):
    vmem = pl.BlockSpec(memory_space=pltpu.VMEM)
    return pl.pallas_call(
        torque_kernel,
        in_specs=[pl.BlockSpec(memory_space=pltpu.SMEM)] + [vmem] * 8,
        out_specs=(vmem, vmem),
        out_shape=(
            jax.ShapeDtypeStruct((SEEN, 3, PLANES, PLANE), F32),
            jax.ShapeDtypeStruct((ROWS, 16, 128), F32),
        ),
        scratch_shapes=[
            pltpu.VMEM((3, PLANES, PLANE), F32),
            pltpu.VMEM((SEEN, 1, PLANE), F32),
            pltpu.VMEM((SEEN, 8, 256), F32),
            pltpu.VMEM((SEEN, 8, 128), F32),
            pltpu.VMEM((SEEN, 8, 128), F32),
        ],
        name="torque",
        compiler_params=pltpu.CompilerParams(vmem_limit_bytes=20 << 20),
    )(at, table, low, high, magnet, below, above, left, right)


def tension_kernel(at_ref, sums_ref, torqued_ref, out_ref, *more):
    cols_at = at_ref[1]
    total = sums_ref[0]
    for r in range(1, ROWS):
        total = total + sums_ref[r]
    total = jnp.sum(total, axis=1, keepdims=True)
    root = jnp.sqrt(total * (1.0 / entries) + 1e-06)
    for p in range(OWN):
        j = p + 1
        coefficient = spring_coef * (root[j + 1 : j + 2] - root[j : j + 1])
        scale = jnp.broadcast_to(coefficient / root[9 + j : 10 + j], (8, 128))
        if p == 0:
            free = cols_at > 0
        elif p == OWN - 1:
            free = cols_at < COLS - 1
        else:
            free = None

        def lanes(k, carry):
            span = pl.ds(pl.multiple_of(128 * k, 128), 128)
            t = [torqued_ref[j, c, :, span] for c in range(3)]
            force = [
                (torqued_ref[j + 1, c, :, span] - torqued_ref[j - 1, c, :, span]) * scale
                for c in range(3)
            ]
            along = force[0] * t[0] + force[1] * t[1] + force[2] * t[2]
            w = [t[c] + force[c] - along * t[c] for c in range(3)]
            size = lax.rsqrt(w[0] * w[0] + w[1] * w[1] + w[2] * w[2])
            for c in range(3):
                new = w[c] * size
                if free is not None:
                    new = jnp.where(free, new, t[c])
                out_ref[c, p, :, span] = new
            return carry

        lax.fori_loop(0, PLANE // 128, lanes, 0, unroll=4)
    if more:
        write_block(at_ref[0], out_ref, *more)


def tension(at, sums, torqued, with_block):
    vmem = pl.BlockSpec(memory_space=pltpu.VMEM)
    block = jax.ShapeDtypeStruct((ROWS, BLOCK, 256), BF16)
    return pl.pallas_call(
        tension_kernel,
        in_specs=[pl.BlockSpec(memory_space=pltpu.SMEM), vmem, vmem],
        out_shape=(jax.ShapeDtypeStruct((3, OWN, PLANES, PLANE), F32),) + ((block,) if with_block else ()),
        scratch_shapes=[pltpu.VMEM((BLOCK, 256), F32)] if with_block else [],
        name="tension",
        compiler_params=pltpu.CompilerParams(vmem_limit_bytes=10 << 20),
    )(at, sums, torqued)


def swap(values, axis):
    return lax.all_to_all(values, axis, split_axis=0, concat_axis=0, tiled=True)


def up(values, axis):
    return lax.ppermute(values, axis, [(i, i + 1) for i in range(lax.axis_size(axis) - 1)])


def down(values, axis):
    return lax.ppermute(values, axis, [(i + 1, i) for i in range(lax.axis_size(axis) - 1)])


def trace_positions(trace_slot, rows_at):
    piece = jnp.minimum(rows_at, COL_BLOCK // PIECE - 1)
    mine = lax.dynamic_slice(
        trace_slot.reshape(COLS, COL_BLOCK), (0, piece * PIECE), (COLS, PIECE)
    )
    high = mine >> 8
    low = mine & 255
    k = (low & 63) >> 1
    odd = low & 1
    far = (low >> 6) & 1
    lane = k + jnp.where(far == 0, odd * 64, 96 - odd * 64)
    low = jnp.where((high < GRID) & (low >= 128), 128 + lane, low)
    return low.reshape(1, COLS * PIECE), high.reshape(1, COLS * PIECE)


def return_positions(return_row, rows_at):
    cycles = lax.dynamic_slice_in_dim(return_row, rows_at * PLANES * 256, PLANES * 256)
    plane = jnp.where(rows_at == 0, return_row[16384:20480], return_row[20480:])
    both = jnp.stack([cycles & 255, cycles >> 8]).reshape(2 * PLANES, 256)
    place = jnp.arange(128, dtype=jnp.int32)
    k = place & 31
    source = jnp.where(
        place < 32, 2 * k, jnp.where(place < 64, 65 + 2 * k, jnp.where(place < 96, 2 * k + 1, 64 + 2 * k))
    )
    order = (source[None, :] == place[:, None]).astype(BF16)
    turned = jnp.dot(both[:, 128:].astype(BF16), order, preferred_element_type=F32).astype(jnp.int32)
    both = jnp.concatenate([both[:, :128], turned], axis=1).reshape(2, PLANES * 256)
    low = jnp.concatenate([both[0], plane & 255])
    high = jnp.concatenate([both[1], plane >> 8])
    return low.reshape(1, -1), high.reshape(1, -1)


def body(m_start, boundary_matrix, trace_slot, return_row):
    rows_at = lax.axis_index("rows")
    cols_at = lax.axis_index("cols")
    at = jnp.stack([rows_at, cols_at]).astype(jnp.int32)
    trace_at = trace_positions(trace_slot, rows_at)
    return_at = return_positions(return_row, rows_at)
    magnet = m_start
    block = surface_block(at, magnet)
    for repeat_at in range(STEPS):
        table = swap(block, "rows")
        from_left = up(magnet[:, OWN - 1], "cols")
        from_right = down(magnet[:, 0], "cols")
        traced = take_trace(table, *trace_at)
        owned = swap(traced, ("rows", "cols"))
        owned, from_left, from_right = lax.optimization_barrier((owned, from_left, from_right))
        head, tail = edge_planes(magnet, from_left, from_right)
        parts = partial_potential(owned, boundary_matrix).astype(jnp.float16)
        parts = swap(parts, "cols").astype(F32)
        below = up(tail, "rows")
        above = down(head, "rows")
        mine, below, above = lax.optimization_barrier((combine(parts), below, above))
        potential = swap(mine, "rows")
        torqued, sums = torque(at, potential, *return_at, magnet, below, above, from_left, from_right)
        sums = swap(sums, "rows")
        made = tension(at, sums, torqued, repeat_at + 1 < STEPS)
        magnet = made[0]
        block = made[-1]
    return magnet


def solution(mesh):
    return jax.shard_map(
        body,
        mesh=mesh,
        in_specs=(P(None, "cols", "rows", None), P("rows", "cols"), P(), P()),
        out_specs=P(None, "cols", "rows", None),
        check_vma=False,
    )
```

```python
import jax
import jax.numpy as jnp
from jax import lax
from jax.experimental import pallas as pl
from jax.experimental.pallas import tpu as pltpu
from jax.sharding import PartitionSpec as P

GRID = 64
STEPS = 2
ROWS = 8
COLS = 16
NB = 24576
PLANES = 8
PLANE = GRID * GRID
COL_BLOCK = NB // COLS
CHUNKS = NB // ROWS // 256
OWN = 4
BLOCK = 144
SEEN = 6
PIECE = 256
WIDE = 1024
F32 = jnp.float32
BF16 = jnp.bfloat16
POT = BF16

exchange_coef = 0.25
demag_coef = 2.0
time_step = 0.2
spring_coef = 2.0
entries = 3.0 * GRID * GRID * GRID


def lanes_of(width):
    return lax.broadcasted_iota(jnp.int32, (8, width), 1)


def neighbours_y(values, before, after):
    width = values.shape[1]
    whole = jnp.concatenate([before, values, after], axis=1)
    pieces = [pltpu.roll(whole[:, 128 * k : 128 * k + 128], 64, 1) for k in range(width // 128 + 2)]
    low = lanes_of(128) < 64
    north = [jnp.where(low, pieces[k + 1], pieces[k + 2]) for k in range(width // 128)]
    south = [jnp.where(low, pieces[k], pieces[k + 1]) for k in range(width // 128)]
    return jnp.concatenate(north, axis=1), jnp.concatenate(south, axis=1)


def neighbours_x(values):
    pieces = [values[:, 128 * k : 128 * k + 128] for k in range(values.shape[1] // 128)]
    east = jnp.concatenate([pltpu.roll(piece, 127, 1) for piece in pieces], axis=1)
    west = jnp.concatenate([pltpu.roll(piece, 1, 1) for piece in pieces], axis=1)
    return east, west


def neighbours_z(values, below, above):
    width = values.shape[1]
    plane = lax.broadcasted_iota(jnp.int32, (8, width), 0)
    upper = jnp.where(plane == 7, jnp.broadcast_to(above, (8, width)), pltpu.roll(values, 7, 0))
    lower = jnp.where(plane == 0, jnp.broadcast_to(below, (8, width)), pltpu.roll(values, 1, 0))
    return upper, lower


def sides(read, chunk):
    start = WIDE * chunk
    centre = read(start, WIDE)
    before = read(start - 128, 128) if chunk > 0 else centre[:, :128]
    after = read(start + WIDE, 128) if start + WIDE < PLANE else centre[:, :128]
    return centre, before, after


def planes_kernel(magnet_ref, left_ref, right_ref, head_ref, tail_ref, stage_ref):
    for z, edge_ref in ((0, head_ref), (7, tail_ref)):
        for i in range(SEEN):
            for c in range(3):
                if i == 0:
                    source = left_ref.at[c]
                elif i == SEEN - 1:
                    source = right_ref.at[c]
                else:
                    source = magnet_ref.at[c, i - 1]
                stage_ref[4 * i + c : 4 * i + c + 1, :] = source[z : z + 1, :]
            stage_ref[4 * i + 3 : 4 * i + 4, :] = jnp.zeros((1, PLANE), F32)
        edge_ref[...] = stage_ref[...].astype(BF16)


def edge_planes(magnet, left, right):
    shape = jax.ShapeDtypeStruct((4 * SEEN, PLANE), BF16)
    return pl.pallas_call(
        planes_kernel,
        out_shape=(shape, shape),
        scratch_shapes=[pltpu.VMEM((4 * SEEN, PLANE), F32)],
        name="edge_planes",
        compiler_params=pltpu.CompilerParams(vmem_limit_bytes=6 << 20),
    )(magnet, left, right)


def three_parts(values):
    top = values.astype(BF16).astype(F32)
    rest = values - top
    middle = rest.astype(BF16).astype(F32)
    return top, middle, rest - middle


def gather_sides(total_x, piece, k, half):
    kept = jnp.where(half == 0, piece, 0.0) + jnp.where(half == 32, pltpu.roll(piece, 33, 1), 0.0)
    return total_x + (pltpu.roll(kept, k, 1) if k else kept)


def write_block(rows_at, magnet_ref, out_ref, stage_ref):
    lane = lanes_of(128)
    half = lane & 63
    for p in range(OWN):
        side_x = jnp.zeros((8, 128), F32)
        side_y = jnp.zeros((8, 128), F32)
        spin_x = jnp.zeros((8, 128), F32)
        spin_y = jnp.zeros((8, 128), F32)
        for chunk in range(PLANE // WIDE):
            span = pl.ds(WIDE * chunk, WIDE)
            wide_lane = lanes_of(WIDE)
            x_at = wide_lane & 63
            y_at = (wide_lane + WIDE * chunk) >> 6
            east, west = neighbours_x(magnet_ref[0, p, :, span])
            north, south = neighbours_y(*sides(lambda s, w: magnet_ref[1, p, :, pl.ds(s, w)], chunk))
            spin = magnet_ref[2, p, :, span]
            nothing = jnp.zeros((1, WIDE), F32)
            upper, lower = neighbours_z(spin, nothing, nothing)
            diverge = 0.5 * (
                jnp.where(x_at < GRID - 1, east, 0.0)
                - jnp.where(x_at > 0, west, 0.0)
                + jnp.where(y_at < GRID - 1, north, 0.0)
                - jnp.where(y_at > 0, south, 0.0)
                + upper
                - lower
            )
            chosen = jnp.where(rows_at == 0, diverge[0:1], diverge[7:8])
            for j in range(WIDE // 256):
                at = 32 + 4 * (chunk * (WIDE // 256) + j) + p
                stage_ref[at : at + 1, :] = chosen[:, 256 * j : 256 * j + 256]
            for j in range(WIDE // 128):
                k = chunk * (WIDE // 128) + j
                side_x = gather_sides(side_x, diverge[:, 128 * j : 128 * j + 128], k, half)
                spin_x = gather_sides(spin_x, spin[:, 128 * j : 128 * j + 128], k, half)
            if chunk == 0:
                side_y = diverge[:, :128]
                spin_y = spin[:, :128]
            if chunk == PLANE // WIDE - 1:
                side_y = jnp.where(lane < 64, side_y, diverge[:, WIDE - 128 :])
                spin_y = jnp.where(lane < 64, spin_y, spin[:, WIDE - 128 :])
        cycle = jnp.concatenate([side_y, side_x], axis=1)
        for z in range(PLANES):
            stage_ref[4 * z + p : 4 * z + p + 1, :] = cycle[z : z + 1]
        parts = three_parts(cycle) + three_parts(jnp.concatenate([spin_y, spin_x], axis=1))
        for n in range(6):
            for end in range(2):
                at = 96 + 24 * end + 4 * n + p
                stage_ref[at : at + 1, :] = parts[n][7 * end : 7 * end + 1]
    whole = stage_ref[...].astype(BF16)
    for r in range(ROWS):
        out_ref[r] = whole


def surface_kernel(at_ref, magnet_ref, out_ref, stage_ref):
    write_block(at_ref[0], magnet_ref, out_ref, stage_ref)


def surface_block(at, magnet):
    return pl.pallas_call(
        surface_kernel,
        in_specs=[pl.BlockSpec(memory_space=pltpu.SMEM), pl.BlockSpec(memory_space=pltpu.VMEM)],
        out_shape=jax.ShapeDtypeStruct((ROWS, BLOCK, 256), BF16),
        scratch_shapes=[pltpu.VMEM((BLOCK, 256), F32)],
        name="surface_block",
        compiler_params=pltpu.CompilerParams(vmem_limit_bytes=8 << 20),
    )(at, magnet)


def lane_choice(low):
    lane = lax.broadcasted_iota(jnp.int32, (256, low.shape[1]), 0)
    return jnp.where(lane == low, 1.0, 0.0).astype(BF16)


def trace_kernel(table_ref, low_ref, high_ref, out_ref, whole_ref):
    ends = [table_ref[slab, 96:BLOCK, :].astype(F32) for slab in range(ROWS)]

    def joined(slab, end, first):
        at = 24 * end + 4 * first
        part = ends[slab]
        return part[at : at + 4] + (part[at + 4 : at + 8] + part[at + 8 : at + 12])

    for slab in range(ROWS):
        base = 32 * slab
        whole_ref[base : base + 32, :] = table_ref[slab, 0:32, :].astype(F32)
        if slab > 0:
            whole_ref[base : base + 4, :] = joined(slab, 0, 0) - 0.5 * joined(slab - 1, 1, 3)
        if slab < ROWS - 1:
            whole_ref[base + 28 : base + 32, :] = joined(slab, 1, 0) + 0.5 * joined(slab + 1, 0, 3)
    whole_ref[256:320, :] = table_ref[0, 32:96, :].astype(F32)
    whole_ref[320:384, :] = table_ref[ROWS - 1, 32:96, :].astype(F32)
    table = whole_ref[...].astype(BF16)
    width = 2 * PIECE
    for tile in range(COLS // 2):
        low = low_ref[:, width * tile : width * tile + width]
        high = high_ref[:, width * tile : width * tile + width]
        picked = jnp.dot(table, lane_choice(low), preferred_element_type=F32)
        offset = high - (lax.broadcasted_iota(jnp.int32, (8, width), 0) >> 2)
        total = jnp.zeros((8, width), F32)
        for pair in range(48):
            total = total + jnp.where(offset == 2 * pair, picked[8 * pair : 8 * pair + 8], 0.0)
        found = (total[0:4] + total[4:8]).astype(BF16)
        for r in range(ROWS):
            out_ref[COLS * r + 2 * tile] = found[:, :PIECE]
            out_ref[COLS * r + 2 * tile + 1] = found[:, PIECE:]


def take_trace(table, low, high):
    return pl.pallas_call(
        trace_kernel,
        out_shape=jax.ShapeDtypeStruct((ROWS * COLS, OWN, PIECE), BF16),
        scratch_shapes=[pltpu.VMEM((384, 256), F32)],
        name="take_trace",
        compiler_params=pltpu.CompilerParams(vmem_limit_bytes=12 << 20),
    )(table, low, high)


def partial_kernel(owned_ref, matrix_ref, out_ref, traced_ref, rows_ref):
    for r in range(COL_BLOCK // PIECE):
        for c in range(COLS):
            traced_ref[OWN * c : OWN * c + OWN, PIECE * r : PIECE * r + PIECE] = owned_ref[
                COLS * r + c
            ].astype(F32)
    traced = traced_ref[...].astype(BF16)
    for side in range(2):
        rows_ref[side, 0:8, :] = jnp.zeros((8, 256), F32)
        rows_ref[side, 72:80, :] = jnp.zeros((8, 256), F32)
    for h in range(CHUNKS):
        rows_ref[h % 2, 8:72, :] = lax.dot_general(
            traced,
            matrix_ref[256 * h : 256 * h + 256, :],
            (((1,), (1,)), ((), ())),
            preferred_element_type=F32,
        )
        for c in range(COLS):
            first = 7 + OWN * c
            for side in range(2):
                at = (2 * h + side) * SEEN
                out_ref[c, at : at + SEEN, :] = rows_ref[
                    h % 2, first : first + SEEN, 128 * side : 128 * side + 128
                ]


def partial_potential(owned, matrix):
    vmem = pl.BlockSpec(memory_space=pltpu.VMEM)
    return pl.pallas_call(
        partial_kernel,
        in_specs=[vmem, vmem],
        out_specs=vmem,
        out_shape=jax.ShapeDtypeStruct((COLS, 2 * CHUNKS * SEEN, 128), F32),
        scratch_shapes=[pltpu.VMEM((64, COL_BLOCK), F32), pltpu.VMEM((2, 80, 256), F32)],
        name="partial_potential",
        compiler_params=pltpu.CompilerParams(vmem_limit_bytes=14 << 20),
    )(owned, matrix)


def combine_kernel(parts_ref, out_ref, sum_ref):
    total = parts_ref[0].astype(F32)
    for c in range(1, COLS):
        total = total + parts_ref[c].astype(F32)
    sum_ref[0 : 2 * CHUNKS * SEEN, :] = total
    sum_ref[2 * CHUNKS * SEEN :, :] = jnp.zeros((8, 128), F32)
    halves = [
        jnp.concatenate(
            [sum_ref[SEEN * (2 * h + side) : SEEN * (2 * h + side) + 8, :] for h in range(CHUNKS)], axis=0
        )
        for side in range(2)
    ]
    rows = jnp.concatenate(halves, axis=1).astype(out_ref.dtype)
    for r in range(ROWS):
        out_ref[r] = rows


def combine(parts):
    return pl.pallas_call(
        combine_kernel,
        out_shape=jax.ShapeDtypeStruct((ROWS, 8 * CHUNKS, 256), POT),
        scratch_shapes=[pltpu.VMEM((2 * CHUNKS * SEEN + 8, 128), F32)],
        name="combine",
        compiler_params=pltpu.CompilerParams(vmem_limit_bytes=6 << 20),
    )(parts)


def exchange_field(rows_at, source_ref, below_ref, above_ref, out_ref):
    for chunk in range(PLANE // WIDE):
        span = pl.ds(WIDE * chunk, WIDE)
        wide_lane = lanes_of(WIDE)
        x_at = wide_lane & 63
        y_at = (wide_lane + WIDE * chunk) >> 6
        centre, before, after = sides(lambda s, w: source_ref[:, pl.ds(s, w)], chunk)
        east, west = neighbours_x(centre)
        north, south = neighbours_y(centre, before, after)
        upper, lower = neighbours_z(
            centre,
            jnp.where(rows_at == 0, centre[0:1], below_ref[:, span]),
            jnp.where(rows_at == ROWS - 1, centre[7:8], above_ref[:, span]),
        )
        total = (
            jnp.where(x_at < GRID - 1, east, centre)
            + jnp.where(x_at > 0, west, centre)
            + jnp.where(y_at < GRID - 1, north, centre)
            + jnp.where(y_at > 0, south, centre)
            + upper
            + lower
        )
        out_ref[:, span] = exchange_coef * (total - 6.0 * centre)


def find_returned(table_ref, low_ref, high_ref, found_ref, cycle_ref):
    table = table_ref[...].reshape(ROWS * 8 * CHUNKS, 256)
    for tile in range(12):
        low = low_ref[:, 512 * tile : 512 * tile + 512]
        high = high_ref[:, 512 * tile : 512 * tile + 512]
        choice = lane_choice(low)
        if POT == BF16:
            picked = jnp.dot(table, choice, preferred_element_type=F32)
        else:
            top = table.astype(BF16)
            rest = (table - top.astype(F32)).astype(BF16)
            picked = jnp.dot(top, choice, preferred_element_type=F32) + jnp.dot(
                rest, choice, preferred_element_type=F32
            )
        high = jnp.broadcast_to(high, (8, 512))
        total = jnp.zeros((8, 512), F32)
        for h in range(ROWS * CHUNKS):
            total = total + jnp.where(high == h, picked[8 * h : 8 * h + 8], 0.0)
        total = demag_coef * total
        if tile < 4:
            for z in range(2):
                for p in range(SEEN):
                    cycle_ref[p, 2 * tile + z : 2 * tile + z + 1, :] = total[
                        p : p + 1, 256 * z : 256 * z + 256
                    ]
        else:
            for p in range(SEEN):
                found_ref[p, :, 512 * (tile - 4) : 512 * (tile - 3)] = total[p : p + 1]


def torque_kernel(
    at_ref, table_ref, low_ref, high_ref, magnet_ref, low_rows, high_rows, left_ref, right_ref,
    out_ref, sums_ref, below_ref, above_ref, field_ref, found_ref, cycle_ref, near_ref, far_ref,
):
    rows_at = at_ref[0]
    for source, rows_ref in ((low_rows, below_ref), (high_rows, above_ref)):
        rows = source[...].astype(F32)
        for i in range(SEEN):
            rows_ref[i] = rows[4 * i : 4 * i + 3]
    find_returned(table_ref, low_ref, high_ref, found_ref, cycle_ref)
    lane = lanes_of(128)
    half = lane & 63
    plane_at = lax.broadcasted_iota(jnp.int32, (8, 128), 0)
    sign = jnp.where(
        (plane_at == 0) & (rows_at == 0),
        1.0,
        jnp.where((plane_at == 7) & (rows_at == ROWS - 1), -1.0, 0.0),
    )

    def image(i, sources):
        for c in range(3):
            exchange_field(
                rows_at, sources[c], below_ref.at[i, c : c + 1], above_ref.at[i, c : c + 1], field_ref.at[c]
            )
        side_y = cycle_ref[i, :, 0:128]
        side_x = cycle_ref[i, :, 128:256]
        near = jnp.zeros((8, 128), F32)
        far = jnp.zeros((8, 128), F32)
        last = jnp.maximum(i - 1, 0)
        second = jnp.maximum(i - 2, 0)
        for k in range(PLANE // 128):
            span = pl.ds(128 * k, 128)
            m = [sources[c][:, span] for c in range(3)]
            f = [field_ref[c, :, span] for c in range(3)]
            rolled = pltpu.roll(side_x, 128 - k, 1) if k else side_x
            f[0] = (
                f[0]
                + jnp.where(half == 0, rolled, 0.0)
                - jnp.where(half == 63, pltpu.roll(side_x, 95 - k, 1), 0.0)
            )
            if k == 0:
                f[1] = f[1] + jnp.where(lane < 64, side_y, 0.0)
            if k == PLANE // 128 - 1:
                f[1] = f[1] - jnp.where(lane >= 64, side_y, 0.0)
            f[2] = f[2] + sign * found_ref[i, :, span]
            along = m[0] * f[0] + m[1] * f[1] + m[2] * f[2]
            length = m[0] * m[0] + m[1] * m[1] + m[2] * m[2]
            v = [m[c] - time_step * (m[c] * along - f[c] * length) for c in range(3)]
            scale = lax.rsqrt(v[0] * v[0] + v[1] * v[1] + v[2] * v[2])
            for c in range(3):
                t = v[c] * scale
                out_ref[i, c, :, span] = t
                step = t - out_ref[last, c, :, span]
                near = near + step * step
                step = t - out_ref[second, c, :, span]
                far = far + step * step
        near_ref[i] = near
        far_ref[i] = far

    def own(i, carry):
        image(i, [magnet_ref.at[c, i - 1] for c in range(3)])
        return carry

    image(0, [left_ref.at[c] for c in range(3)])
    lax.fori_loop(1, SEEN - 1, own, 0)
    image(SEEN - 1, [right_ref.at[c] for c in range(3)])
    blank = jnp.zeros((2, 128), F32)
    sums = jnp.concatenate(
        [jnp.sum(near_ref[n], axis=0, keepdims=True) for n in range(SEEN)]
        + [blank]
        + [jnp.sum(far_ref[n], axis=0, keepdims=True) for n in range(SEEN)]
        + [blank],
        axis=0,
    )
    for r in range(ROWS):
        sums_ref[r] = sums


def torque(at, table, low, high, magnet, below, above, left, right):
    vmem = pl.BlockSpec(memory_space=pltpu.VMEM)
    return pl.pallas_call(
        torque_kernel,
        in_specs=[pl.BlockSpec(memory_space=pltpu.SMEM)] + [vmem] * 8,
        out_specs=(vmem, vmem),
        out_shape=(
            jax.ShapeDtypeStruct((SEEN, 3, PLANES, PLANE), F32),
            jax.ShapeDtypeStruct((ROWS, 16, 128), F32),
        ),
        scratch_shapes=[
            pltpu.VMEM((SEEN, 3, PLANE), F32),
            pltpu.VMEM((SEEN, 3, PLANE), F32),
            pltpu.VMEM((3, PLANES, PLANE), F32),
            pltpu.VMEM((SEEN, 1, PLANE), F32),
            pltpu.VMEM((SEEN, 8, 256), F32),
            pltpu.VMEM((SEEN, 8, 128), F32),
            pltpu.VMEM((SEEN, 8, 128), F32),
        ],
        name="torque",
        compiler_params=pltpu.CompilerParams(vmem_limit_bytes=20 << 20),
    )(at, table, low, high, magnet, below, above, left, right)


def tension_kernel(at_ref, sums_ref, torqued_ref, out_ref, *more):
    cols_at = at_ref[1]
    total = sums_ref[0]
    for r in range(1, ROWS):
        total = total + sums_ref[r]
    total = jnp.sum(total, axis=1, keepdims=True)
    root = jnp.sqrt(total * (1.0 / entries) + 1e-06)
    for p in range(OWN):
        j = p + 1
        coefficient = spring_coef * (root[j + 1 : j + 2] - root[j : j + 1])
        scale = jnp.broadcast_to(coefficient / root[9 + j : 10 + j], (8, 128))
        if p == 0:
            free = cols_at > 0
        elif p == OWN - 1:
            free = cols_at < COLS - 1
        else:
            free = None

        def lanes(k, carry):
            span = pl.ds(pl.multiple_of(128 * k, 128), 128)
            t = [torqued_ref[j, c, :, span] for c in range(3)]
            force = [
                (torqued_ref[j + 1, c, :, span] - torqued_ref[j - 1, c, :, span]) * scale
                for c in range(3)
            ]
            along = force[0] * t[0] + force[1] * t[1] + force[2] * t[2]
            w = [t[c] + force[c] - along * t[c] for c in range(3)]
            size = lax.rsqrt(w[0] * w[0] + w[1] * w[1] + w[2] * w[2])
            for c in range(3):
                new = w[c] * size
                if free is not None:
                    new = jnp.where(free, new, t[c])
                out_ref[c, p, :, span] = new
            return carry

        lax.fori_loop(0, PLANE // 128, lanes, 0, unroll=4)
    if more:
        write_block(at_ref[0], out_ref, *more)


def tension(at, sums, torqued, with_block):
    vmem = pl.BlockSpec(memory_space=pltpu.VMEM)
    block = jax.ShapeDtypeStruct((ROWS, BLOCK, 256), BF16)
    return pl.pallas_call(
        tension_kernel,
        in_specs=[pl.BlockSpec(memory_space=pltpu.SMEM), vmem, vmem],
        out_shape=(jax.ShapeDtypeStruct((3, OWN, PLANES, PLANE), F32),) + ((block,) if with_block else ()),
        scratch_shapes=[pltpu.VMEM((BLOCK, 256), F32)] if with_block else [],
        name="tension",
        compiler_params=pltpu.CompilerParams(vmem_limit_bytes=10 << 20),
    )(at, sums, torqued)


def swap(values, axis):
    return lax.all_to_all(values, axis, split_axis=0, concat_axis=0, tiled=True)


def up(values, axis):
    return lax.ppermute(values, axis, [(i, i + 1) for i in range(lax.axis_size(axis) - 1)])


def down(values, axis):
    return lax.ppermute(values, axis, [(i + 1, i) for i in range(lax.axis_size(axis) - 1)])


def trace_positions(trace_slot, rows_at):
    piece = jnp.minimum(rows_at, COL_BLOCK // PIECE - 1)
    mine = lax.dynamic_slice(
        trace_slot.reshape(COLS, COL_BLOCK), (0, piece * PIECE), (COLS, PIECE)
    )
    high = mine >> 8
    low = mine & 255
    k = (low & 63) >> 1
    odd = low & 1
    far = (low >> 6) & 1
    lane = k + jnp.where(far == 0, odd * 64, 96 - odd * 64)
    low = jnp.where((high < GRID) & (low >= 128), 128 + lane, low)
    return low.reshape(1, COLS * PIECE), high.reshape(1, COLS * PIECE)


def return_positions(return_row, rows_at):
    cycles = lax.dynamic_slice_in_dim(return_row, rows_at * PLANES * 256, PLANES * 256)
    plane = jnp.where(rows_at == 0, return_row[16384:20480], return_row[20480:])
    both = jnp.stack([cycles & 255, cycles >> 8]).reshape(2 * PLANES, 256)
    place = jnp.arange(128, dtype=jnp.int32)
    k = place & 31
    source = jnp.where(
        place < 32, 2 * k, jnp.where(place < 64, 65 + 2 * k, jnp.where(place < 96, 2 * k + 1, 64 + 2 * k))
    )
    order = (source[None, :] == place[:, None]).astype(BF16)
    turned = jnp.dot(both[:, 128:].astype(BF16), order, preferred_element_type=F32).astype(jnp.int32)
    both = jnp.concatenate([both[:, :128], turned], axis=1).reshape(2, PLANES * 256)
    low = jnp.concatenate([both[0], plane & 255])
    high = jnp.concatenate([both[1], plane >> 8])
    return low.reshape(1, -1), high.reshape(1, -1)


def body(m_start, boundary_matrix, trace_slot, return_row):
    rows_at = lax.axis_index("rows")
    cols_at = lax.axis_index("cols")
    at = jnp.stack([rows_at, cols_at]).astype(jnp.int32)
    trace_at = trace_positions(trace_slot, rows_at)
    return_at = return_positions(return_row, rows_at)
    magnet = m_start
    block = surface_block(at, magnet)
    for repeat_at in range(STEPS):
        table = swap(block, "rows")
        from_left = up(magnet[:, OWN - 1], "cols")
        from_right = down(magnet[:, 0], "cols")
        traced = take_trace(table, *trace_at)
        owned = swap(traced, ("rows", "cols"))
        owned, from_left, from_right = lax.optimization_barrier((owned, from_left, from_right))
        head, tail = edge_planes(magnet, from_left, from_right)
        parts = partial_potential(owned, boundary_matrix).astype(jnp.float16)
        parts = swap(parts, "cols").astype(F32)
        below = up(tail, "rows")
        above = down(head, "rows")
        mine, below, above = lax.optimization_barrier((combine(parts), below, above))
        potential = swap(mine, "rows")
        torqued, sums = torque(at, potential, *return_at, magnet, below, above, from_left, from_right)
        sums = swap(sums, "rows")
        made = tension(at, sums, torqued, repeat_at + 1 < STEPS)
        magnet = made[0]
        block = made[-1]
    return magnet


def solution(mesh):
    return jax.shard_map(
        body,
        mesh=mesh,
        in_specs=(P(None, "cols", "rows", None), P("rows", "cols"), P(), P()),
        out_specs=P(None, "cols", "rows", None),
        check_vma=False,
    )
```
